32 devices in a mesh: slab: 8 (over z, x), pencil: 4 (over y, core).
Axes of the slice: x: 2, y: 2, z: 4, core: 2. Of those that a mesh axis runs over, the one named last changes fastest.
Arguments:
- a_blocks: float32 [128, 32, 20480], P('slab', 'pencil'), may hold values from -1 to 8, as said below
- col_codes: int32 [128, 32, 5], P('slab', 'pencil'), may hold values from 0 to 8, as said below
- agg_of: int32 [128, 32], P('slab', 'pencil'), may hold values from 0 to 511, as said below
- test_vectors: float32 [128, 32, 2048], P('slab', 'pencil'), may hold values from -36 to 36
Outputs:
- relaxed: float32 [128, 32, 2048], P('slab', 'pencil')
- tiles: float32 [128, 32, 512], P('slab', 'pencil')
- products: float32 [128, 32, 2560], P('slab', 'pencil')
The draws below stay inside these ranges and needn't reach their ends.
Inputs may be any that keep to these rules, and one draw needn't show every extreme that they name: `col_codes`: slot 0 of every block row is code 4, the block row itself; slots 1 to 4 hold different codes among the other eight of the 3 x 3 neighbourhood. `agg_of`: aggregate g is owned by device g // 16, devices numbered slab-major. On each device the block rows, in row-major order, form 16 groups of 8 consecutive block rows; all block rows of a group belong to aggregates of one owner, and the groups of one device go to different owners. Some owners receive a group from every device. `a_blocks`: the diagonal entries of every slot-0 block lie in [1.99, 8].
All inputs are finite; a program needn't handle non-finite values.
Results may differ from the reference program's by a relative error of at most 0.0003.
Values sent between devices are 32-bit elements; how exact they have to be, the bound alone decides.
No kernel may reach another device: no remote copies, remote signals or barrier semaphores. Data moves between devices by JAX's collectives and lax.ppermute only.
A program may use at most 320 MiB of HBM per device.

```python
import math
import jax
import jax.numpy as jnp
from jax import lax

BLK = 64
NV = 32
NC = 8
KS = 5
ITERS = 2
BS_DEV = 16
BP_DEV = 8
NBS = 128
NBP = 32
CAP = 8
GROUPS = 16
HOT = 2
AGG_DEV = 16
NAGG = 512


def draw_a_blocks(key, part):
    off_key, diag_key = jax.random.split(jax.random.fold_in(key, 7))
    offdiag = 0.05 * jax.random.normal(off_key, (NBS, NBP, KS, BLK, BLK), jnp.float32)
    diagonal = jnp.exp(jax.random.uniform(diag_key, (NBS, NBP, BLK), jnp.float32, 0.6931, 2.0794))
    identity = jnp.eye(BLK, dtype=jnp.float32)
    self_block = offdiag[:, :, 0] * (1.0 - identity) + diagonal[:, :, :, None] * identity
    whole = jnp.concatenate([self_block[:, :, None], offdiag[:, :, 1:]], axis=2)
    return whole.reshape(NBS, NBP, KS * BLK * BLK).astype(jnp.float32)


def draw_col_codes(key, part):
    scores = jax.random.randint(jax.random.fold_in(key, 5), (NBS, NBP, 8), 0, 1024) * 16 + jnp.arange(8, dtype=jnp.int32)
    ranked = jnp.argsort(-scores, axis=-1)[:, :, :KS - 1].astype(jnp.int32)
    others = jnp.where(ranked < 4, ranked, ranked + 1)
    centre = jnp.full((NBS, NBP, 1), 4, jnp.int32)
    return jnp.concatenate([centre, others], axis=-1).astype(jnp.int32)


def draw_agg_of(key, part):
    n_slab = NBS // BS_DEV
    n_pencil = NBP // BP_DEV
    devices = n_slab * n_pencil
    rows_dev = BS_DEV * BP_DEV
    hot_key, dev_key = jax.random.split(jax.random.fold_in(key, 11))
    hot_scores = jax.random.randint(hot_key, (devices,), 0, 4096) * devices + jnp.arange(devices, dtype=jnp.int32)
    hot_rank = jnp.argsort(jnp.argsort(-hot_scores))
    is_hot = (hot_rank < HOT).astype(jnp.int32)

    def one_device(dev_seed):
        score_key, order_key, local_key = jax.random.split(dev_seed, 3)
        scores = jax.random.randint(score_key, (devices,), 0, 4096) * devices + jnp.arange(devices, dtype=jnp.int32) + is_hot * (4096 * devices)
        chosen = jnp.argsort(-scores)[:GROUPS].astype(jnp.int32)
        owners = chosen[jax.random.permutation(order_key, GROUPS)]
        local = jax.random.randint(local_key, (GROUPS, CAP), 0, AGG_DEV)
        return (owners[:, None] * AGG_DEV + local).reshape(rows_dev)
    device_share = jax.vmap(one_device)(jax.random.split(dev_key, devices))
    grid = device_share.reshape(n_slab, n_pencil, BS_DEV, BP_DEV)
    return grid.transpose(0, 2, 1, 3).reshape(NBS, NBP).astype(jnp.int32)


def draw_test_vectors(key, part):
    base_key = jax.random.fold_in(jax.random.fold_in(key, 3), 0)
    rising = 1.0 + 2.0 * jnp.arange(NBS, dtype=jnp.float32) / max(NBS - 1, 1)
    values = jnp.clip(jax.random.normal(base_key, (NBS, NBP, BLK * NV), jnp.float32), -6.0, 6.0)
    return (values * rising[:, None, None]).astype(jnp.float32)


def setup_inputs(seed: int = 0) -> dict:
    arg_keys = jax.random.split(jax.random.key(seed), 5)
    a_blocks = draw_a_blocks(jax.random.fold_in(arg_keys[4], 71), 0)
    col_codes = draw_col_codes(jax.random.fold_in(arg_keys[4], 71), 0)
    agg_of = draw_agg_of(jax.random.fold_in(arg_keys[4], 71), 0)
    test_vectors = draw_test_vectors(jax.random.fold_in(arg_keys[4], 71), 0)
    return {"a_blocks": a_blocks, "col_codes": col_codes, "agg_of": agg_of, "test_vectors": test_vectors}


OMEGA = 2.0 / 3.0
FULL_PRECISION = lax.Precision.HIGHEST

def coarse_modes(cells, coarse):
    centre = jnp.arange(cells, dtype=jnp.float32) + 0.5
    order = jnp.arange(coarse, dtype=jnp.float32)
    return jnp.cos(math.pi * centre[:, None] * order[None, :] / cells)

def solve_maps(coarse):
    gram = jnp.einsum('gkv,glv->gkl', coarse, coarse, precision=FULL_PRECISION)
    trace_sum = jnp.trace(gram, axis1=1, axis2=2)
    ridge = 0.1 * trace_sum / NC + 1e-06
    gram = gram + ridge[:, None, None] * jnp.eye(NC, dtype=jnp.float32)[None]
    lower = jnp.linalg.cholesky(gram)
    half_solved = jax.scipy.linalg.solve_triangular(lower, coarse, lower=True)
    solved = jax.scipy.linalg.solve_triangular(lower, half_solved, lower=True, trans=1)
    return jnp.swapaxes(solved, 1, 2)

def apply_rows(blocks, field, col_codes, form):
    padded = jnp.pad(field, ((1, 1), (1, 1), (0, 0), (0, 0)))
    across_index = jnp.arange(NBP, dtype=jnp.int32)

    def one_row(row_index):
        window = lax.dynamic_slice_in_dim(padded, row_index, 3, 0)
        codes = lax.dynamic_index_in_dim(col_codes, row_index, 0, keepdims=False)
        row_blocks = lax.dynamic_index_in_dim(blocks, row_index, 0, keepdims=False)
        picked = window[codes // 3, across_index[:, None] + codes % 3]
        return jnp.einsum(form, row_blocks, picked, precision=FULL_PRECISION)
    return lax.map(one_row, jnp.arange(NBS, dtype=jnp.int32))

def reference(a_blocks, col_codes, agg_of, test_vectors):
    blocks = a_blocks.reshape(NBS, NBP, KS, BLK, BLK)
    diagonal = jnp.diagonal(blocks[:, :, 0], axis1=-2, axis2=-1)
    candidate_vectors = test_vectors.reshape(NBS, NBP, BLK, NV)
    for sweep in range(ITERS):
        image = apply_rows(blocks, candidate_vectors, col_codes, 'jkoc,jkcw->jow')
        candidate_vectors = candidate_vectors - OMEGA * image / diagonal[:, :, :, None]
    squares = lax.optimization_barrier(jnp.sum(candidate_vectors * candidate_vectors, axis=(0, 1, 2)))
    scale = jnp.sqrt(squares / (NBS * NBP * BLK) + 1e-06)
    relaxed = candidate_vectors / scale
    near_null_modes = coarse_modes(BLK, NC)
    flat_rows = relaxed.reshape(NBS * NBP, BLK, NV)
    coef = jnp.einsum('ck,rcv->rkv', near_null_modes, flat_rows, precision=FULL_PRECISION)
    agg_ids = agg_of.reshape(-1)
    counts = jax.ops.segment_sum(jnp.ones(agg_ids.shape, jnp.float32), agg_ids, num_segments=NAGG)
    summed = jax.ops.segment_sum(coef, agg_ids, num_segments=NAGG)
    coarse = summed / jnp.maximum(counts, 1.0)[:, None, None]
    maps = solve_maps(coarse)
    tile_rows = jnp.einsum('rcv,rvk->rck', flat_rows, maps[agg_ids], precision=FULL_PRECISION)
    tile_grid = tile_rows.reshape(NBS, NBP, BLK, NC)
    products = apply_rows(blocks, tile_grid, col_codes, 'jkoc,jkcw->jkow')
    return (relaxed.reshape(NBS, NBP, BLK * NV), tile_grid.reshape(NBS, NBP, BLK * NC), products.reshape(NBS, NBP, KS * BLK * NC))
```

```python
import functools
import math

import jax
import jax.numpy as jnp
import numpy as np
from jax import lax
from jax.experimental import pallas as pl
from jax.experimental.pallas import tpu as pltpu
from jax.sharding import PartitionSpec as P

BLK = 64
NV = 32
NC = 8
KS = 5
ITERS = 2
OMEGA = 2.0 / 3.0
LANES = 128
F32 = jnp.float32
BF16 = jnp.bfloat16
PAIRS = BLK // 2
VROWS = BLK * NV // LANES
TROWS = BLK * NC // LANES
VM = pl.BlockSpec(memory_space=pltpu.VMEM)
SM = pl.BlockSpec(memory_space=pltpu.SMEM)
HB = pl.BlockSpec(memory_space=pl.ANY)
LIMIT = 48 * 1024 * 1024


def lane_iota(rows):
    return lax.broadcasted_iota(jnp.int32, (rows, LANES), 1)


def row_iota(rows):
    return lax.broadcasted_iota(jnp.int32, (rows, LANES), 0)


def roll(x, shift):
    return pltpu.roll(x, shift, 1)


def upper(x):
    return x.astype(BF16).astype(F32)


def hi_lo_lanes(x):
    return x - jnp.where(lane_iota(x.shape[0]) < 64, 0.0, upper(x))


def put_weights(pairs, rep_ref, w_ref, index, half):
    low = (lane_iota(PAIRS) & half) == 0
    turned = roll(pairs, half)
    rep_ref[pl.ds(0, PAIRS, stride=2), :] = jnp.where(low, pairs, turned)
    rep_ref[pl.ds(1, PAIRS, stride=2), :] = jnp.where(low, turned, pairs)
    y = hi_lo_lanes(rep_ref[...])
    low = (lane_iota(BLK) & half) == 0
    w_ref[index, 0:BLK, :] = jnp.where(low, y, 0.0).astype(BF16)
    w_ref[index, BLK : 2 * BLK, :] = jnp.where(low, 0.0, y).astype(BF16)


def rows_to_pairs(rows, out_ref, start):
    low = lane_iota(VROWS) < 64
    turned = roll(rows, 64)
    out_ref[pl.ds(start, VROWS, stride=2), :] = jnp.where(low, rows, turned)
    out_ref[pl.ds(start + 1, VROWS, stride=2), :] = jnp.where(low, turned, rows)


def pairs_to_rows(ref, start):
    even = ref[pl.ds(start, VROWS, stride=2), :]
    odd = ref[pl.ds(start + 1, VROWS, stride=2), :]
    return jnp.where(lane_iota(VROWS) < 64, even, odd)


def mm(a, b):
    return jnp.dot(a, b, preferred_element_type=F32)


def fold_rows(parts):
    sub = row_iota(8)
    step = 4
    while len(parts) > 1:
        half = len(parts) // 2
        parts = [
            jnp.where(
                (sub & step) == 0,
                parts[u] + pltpu.roll(parts[u], 8 - step, 0),
                parts[u + half] + pltpu.roll(parts[u + half], step, 0),
            )
            for u in range(half)
        ]
        step //= 2
    return parts[0]


def neighbour(codes_ref, b, i, j, k, wide):
    if k == 0:
        return (i + 1) * wide + j + 1
    c = codes_ref[b * KS + k]
    return (i + c // 3) * wide + j + c % 3


def prepare_kernel(height, across, meta_ref, a_hbm, tv_ref, ones_ref, hl_ref, rd_ref, v_ref, buf, sem):
    tiles = KS * PAIRS
    chunk = tiles * across
    depth = buf.shape[0]

    def copy(i):
        slot = lax.rem(i, depth)
        return pltpu.make_async_copy(
            a_hbm.at[pl.ds(i * chunk, chunk), :], buf.at[slot], sem.at[slot]
        )

    for i in range(depth - 1):
        copy(i).start()
    lane = lane_iota(PAIRS)
    on_diagonal = (lane & 63) == 2 * row_iota(PAIRS) + (lane >> 6)

    def body(i, carry):
        @pl.when(i + depth - 1 < height)
        def _():
            copy(i + depth - 1).start()

        copy(i).wait()
        slot = lax.rem(i, depth)
        for j in range(across):
            b = i * across + j
            rows_to_pairs(
                tv_ref[pl.ds(i * VROWS * across + j, VROWS, stride=across), :], v_ref, b * PAIRS
            )
            for k in range(KS):
                x = buf[slot, pl.ds(k * PAIRS * across + j, PAIRS, stride=across), :]
                hi = x.astype(BF16)
                lo = (x - hi.astype(F32)).astype(BF16)
                hl_ref[b, 0:PAIRS, k * LANES : (k + 1) * LANES] = hi
                hl_ref[b, PAIRS : 2 * PAIRS, k * LANES : (k + 1) * LANES] = lo
                if k == 0:
                    d = jnp.where(on_diagonal, x, 0.0)
                    d_hi = d.astype(BF16)
                    d_lo = (d - d_hi.astype(F32)).astype(BF16)
                    s = mm(jnp.concatenate([d_hi, d_lo], axis=0), ones_ref[...])
                    rd_ref[pl.ds(b * PAIRS, PAIRS), :] = OMEGA / (s[:PAIRS] + s[PAIRS:])
        return carry

    lax.fori_loop(0, height, body, 0)


def halo_slots(meta_ref, height, across):
    slab_odd, pencil_odd = meta_ref[0], meta_ref[1]
    col_a = jnp.where(pencil_odd == 0, across + 1, 0)
    row_a = jnp.where(slab_odd == 0, height + 1, 0)
    return row_a, height + 1 - row_a, col_a, across + 1 - col_a


def sweep_core(height, across, codes_ref, meta_ref, hl_ref, rd_ref, v_ref, halo, w_ref, rep_ref, tmp_ref, store):
    wide = across + 2
    pa_ref, pb_ref, sa_ref, sb_ref = halo
    row_a, row_b, col_a, col_b = halo_slots(meta_ref, height, across)

    def own(i, carry):
        for j in range(across):
            put_weights(
                v_ref[pl.ds((i * across + j) * PAIRS, PAIRS), :],
                rep_ref.at[j], w_ref, (i + 1) * wide + j + 1, NV,
            )
        for s, (ref, col) in enumerate(((pa_ref, col_a), (pb_ref, col_b))):
            rows_to_pairs(ref[pl.ds(i * VROWS, VROWS), :], tmp_ref.at[s], 0)
            put_weights(tmp_ref[s], rep_ref.at[s], w_ref, (i + 1) * wide + col, NV)
        return carry

    lax.fori_loop(0, height, own, 0)
    for s, (ref, row) in enumerate(((sa_ref, row_a), (sb_ref, row_b))):
        for j in range(wide):
            col = j + 1 if j < across else (col_a if j == across else col_b)
            q = (s * wide + j) % across
            rows_to_pairs(ref[j * VROWS : (j + 1) * VROWS, :], tmp_ref.at[q], 0)
            put_weights(tmp_ref[q], rep_ref.at[q], w_ref, row * wide + col, NV)

    def body(i, carry):
        for j in range(across):
            b = i * across + j
            w = jnp.concatenate(
                [w_ref[neighbour(codes_ref, b, i, j, k, wide)] for k in range(KS)], axis=0
            )
            r = mm(hl_ref[b], w)
            s = r[:PAIRS] + r[PAIRS:]
            s = s + roll(s, 64)
            at = pl.ds(b * PAIRS, PAIRS)
            store(i, j, b, v_ref[at, :] - s * rd_ref[at, :])
        return carry

    lax.fori_loop(0, height, body, 0)


def sweep_kernel(height, across, codes_ref, meta_ref, hl_ref, rd_ref, v_ref, pa, pb, sa, sb,
                 out_ref, ea_ref, eb_ref, ra_ref, rb_ref, w_ref, rep_ref, tmp_ref):
    def store(i, j, b, value):
        out_ref[pl.ds(b * PAIRS, PAIRS), :] = value

    sweep_core(height, across, codes_ref, meta_ref, hl_ref, rd_ref, v_ref, (pa, pb, sa, sb),
               w_ref, rep_ref, tmp_ref, store)
    row_a, row_b, col_a, col_b = halo_slots(meta_ref, height, across)

    def edge(i, carry):
        for ref, col in ((ea_ref, col_a), (eb_ref, col_b)):
            j = jnp.where(col == 0, 0, across - 1)
            ref[pl.ds(i * VROWS, VROWS), :] = pairs_to_rows(out_ref, (i * across + j) * PAIRS)
        return carry

    lax.fori_loop(0, height, edge, 0)
    for ref, row in ((ra_ref, row_a), (rb_ref, row_b)):
        i = jnp.where(row == 0, 0, height - 1)
        for j in range(across):
            ref[j * VROWS : (j + 1) * VROWS, :] = pairs_to_rows(out_ref, (i * across + j) * PAIRS)


def last_sweep_kernel(height, across, capacity, codes_ref, meta_ref, owner_ref, hl_ref, rd_ref, v_ref,
                      pa, pb, sa, sb, ids_ref, modes_ref, out_ref, pay_ref, w_ref, rep_ref, tmp_ref,
                      coef_ref):
    devices = ids_ref.shape[0]
    hcount = -(-capacity // 4)
    slot_rows = hcount * NC + 1

    def store(i, j, b, value):
        out_ref[pl.ds(b * PAIRS, PAIRS), :] = value

    sweep_core(height, across, codes_ref, meta_ref, hl_ref, rd_ref, v_ref, (pa, pb, sa, sb),
               w_ref, rep_ref, tmp_ref, store)
    pay_ref[...] = jnp.zeros(pay_ref.shape, F32)
    low = (lane_iota(NC) & NV) == 0
    modes = modes_ref[...]
    group_lane = lane_iota(NC) // NV

    def coefs(i, acc):
        for j in range(across):
            b = i * across + j
            v = out_ref[pl.ds(b * PAIRS, PAIRS), :]
            acc = acc + v * v
            r = mm(modes, hi_lo_lanes(v).astype(BF16))
            c = jnp.where(low, r[0:8] + r[16:24], r[8:16] + r[24:32])
            c = c + roll(c, NV)
            coef_ref[pl.ds(b * NC, NC), :] = c + roll(c, 64)
        return acc

    acc = lax.fori_loop(0, height, coefs, jnp.zeros((PAIRS, LANES), F32))
    total = jnp.sum(acc, axis=0, keepdims=True)
    total = total + roll(total, NV)
    pay_ref[pl.ds(slot_rows - 1, devices, stride=slot_rows), :] = jnp.where(
        lane_iota(devices) < NV, total, ids_ref[...]
    )

    def pack(g, carry):
        owner = owner_ref[g]
        for h in range(hcount):
            parts = [
                coef_ref[pl.ds((g * capacity + h * 4 + s) * NC, NC), :]
                for s in range(min(4, capacity - h * 4))
            ]
            c = jnp.zeros((NC, LANES), F32)
            for s, part in enumerate(parts):
                c = jnp.where(group_lane == s, part, c)
            pay_ref[pl.ds(owner * slot_rows + h * NC, NC), :] = c
        return carry

    lax.fori_loop(0, height * across // capacity, pack, 0)


def solve_kernel(cells, per_owner, capacity, got_ref, ret_ref, inv_ref):
    hcount = -(-capacity // 4)
    slot_rows = hcount * NC + 1
    devices = got_ref.shape[0] // slot_rows
    lane = lane_iota(devices)
    extra = got_ref[pl.ds(slot_rows - 1, devices, stride=slot_rows), :]
    total = jnp.sum(jnp.where(lane < NV, extra, 0.0), axis=0, keepdims=True)
    total = jnp.broadcast_to(total, (8, LANES))
    total = total + roll(total, NV)
    total = total + roll(total, 64)
    inv = 1.0 / jnp.sqrt(total / cells + 1e-06)
    inv_ref[...] = inv
    width = 4 * per_owner
    inner = lane & (width - 1)
    hot = []
    for h in range(hcount):
        want = jnp.full((devices, LANES), -1.0, F32)
        for s in range(min(4, capacity - 4 * h)):
            column = extra[:, NV + 4 * h + s : NV + 4 * h + s + 1]
            want = jnp.where(inner // per_owner == s, column, want)
        same = want == (inner & (per_owner - 1)).astype(F32)
        hot.append(jnp.where(same & (lane < 2 * width), 1.0, 0.0))
    hot = jnp.concatenate(hot, axis=0)
    hot_t = jnp.transpose(hot)[:width]
    parts = [
        jnp.concatenate(
            [got_ref[pl.ds(h * NC + m, devices, stride=slot_rows), :] for h in range(hcount)], axis=0
        )
        for m in range(NC)
    ]
    data = jnp.concatenate(parts, axis=1)
    ones = jnp.ones((hcount * devices, LANES), F32)
    high = jnp.concatenate([data, ones], axis=1).astype(BF16)
    rest = jnp.concatenate([data - upper(data), jnp.zeros_like(ones)], axis=1).astype(BF16)
    hot_b = hot_t.astype(BF16)
    sums = mm(hot_b, high) + mm(hot_b, rest)
    group_lane = lane_iota(per_owner) // NV

    def block(s, m):
        return sums[s * per_owner : (s + 1) * per_owner, m * LANES : (m + 1) * LANES]

    count = sum(block(s, NC) for s in range(4))
    weight = inv[0:1] / jnp.maximum(count, 1.0)
    coarse = []
    for m in range(NC):
        c = jnp.zeros((per_owner, LANES), F32)
        for s in range(4):
            c = jnp.where(group_lane == s, block(s, m), c)
        c = c + roll(c, NV)
        c = c + roll(c, 64)
        coarse.append(c * weight)

    def dot_all(x):
        for shift in (16, 8, 4, 2, 1):
            x = x + roll(x, shift)
        return x

    gram = {(a, c): dot_all(coarse[a] * coarse[c]) for a in range(NC) for c in range(a + 1)}
    ridge = 0.1 * sum(gram[m, m] for m in range(NC)) / NC + 1e-06
    for m in range(NC):
        gram[m, m] = gram[m, m] + ridge
    recip = []
    for m in range(NC):
        root = 1.0 / jnp.sqrt(gram[m, m])
        recip.append(root)
        for a in range(m + 1, NC):
            gram[a, m] = gram[a, m] * root
        for a in range(m + 1, NC):
            for c in range(m + 1, a + 1):
                gram[a, c] = gram[a, c] - gram[a, m] * gram[c, m]
    solved = list(coarse)
    for m in range(NC):
        solved[m] = solved[m] * recip[m]
        for a in range(m + 1, NC):
            solved[a] = solved[a] - gram[a, m] * solved[m]
    for m in reversed(range(NC)):
        solved[m] = solved[m] * recip[m]
        for a in range(m):
            solved[a] = solved[a] - gram[m, a] * solved[m]
    table = jnp.concatenate(
        [
            jnp.concatenate([jnp.where(group_lane == s, solved[m], 0.0) for s in range(4)], axis=0)
            for m in range(NC)
        ],
        axis=1,
    )
    stacked = jnp.concatenate([table.astype(BF16), (table - upper(table)).astype(BF16)], axis=0)
    back = mm(hot[:, : 2 * width].astype(BF16), stacked)
    for h in range(hcount):
        for m in range(NC):
            ret_ref[pl.ds(h * NC + m, devices, stride=hcount * NC), :] = back[
                h * devices : (h + 1) * devices, m * LANES : (m + 1) * LANES
            ]


def relaxed_kernel(height, across, v_ref, inv_ref, rel_ref, left_ref):
    inv = inv_ref[0:1, :]

    def body(i, carry):
        for j in range(across):
            b = i * across + j
            rel_ref[pl.ds(i * VROWS * across + j, VROWS, stride=across), :] = (
                pairs_to_rows(v_ref, b * PAIRS) * inv
            )
            left_ref[b] = hi_lo_lanes(v_ref[pl.ds(b * PAIRS, PAIRS), :] * inv).astype(BF16)
        return carry

    lax.fori_loop(0, height, body, 0)


def tile_kernel(height, across, capacity, meta_ref, owner_ref, ret_ref, left_ref,
                pairs_ref, out_ref, ea_ref, eb_ref, ra_ref, rb_ref):
    hcount = -(-capacity // 4)
    low = (lane_iota(NC) & NV) == 0
    group_lane = lane_iota(NC) // NV
    picks = lane_iota(8) // 16 == row_iota(8)

    def body(i, carry):
        tiles = []
        for j in range(across):
            b = i * across + j
            g = b // capacity
            inner = b - g * capacity
            owner = owner_ref[g]
            h, s = inner // 4, inner % 4
            m = ret_ref[pl.ds(pl.multiple_of((owner * hcount + h) * NC, NC), NC), :]
            m = jnp.where(group_lane == s, m, 0.0)
            m = m + roll(m, NV)
            m = m + roll(m, 64)
            m_hi = upper(m)
            halves = []
            for part in (m_hi, m - m_hi):
                both = jnp.concatenate(
                    [jnp.where(low, part, 0.0), jnp.where(low, 0.0, part)], axis=0
                ).astype(BF16)
                halves.append(jnp.concatenate([both] * 8, axis=0))
            left = left_ref[b]
            t = lax.dot_general(
                jnp.concatenate([left, left], axis=1),
                jnp.concatenate(halves, axis=1),
                (((1,), (1,)), ((), ())),
                preferred_element_type=F32,
            )
            pairs_ref[pl.ds(b * PAIRS, PAIRS), :] = t
            tiles.append(t)
        for q in range(TROWS):
            rows = fold_rows([jnp.where(picks, t[q * 8 : (q + 1) * 8], 0.0) for t in tiles])
            out_ref[pl.ds((i * TROWS + q) * across, across), :] = rows
        return carry

    lax.fori_loop(0, height, body, 0)
    row_a, row_b, col_a, col_b = halo_slots(meta_ref, height, across)
    for ref, col in ((ea_ref, col_a), (eb_ref, col_b)):
        j = jnp.where(col == 0, 0, across - 1)
        ref[...] = out_ref[pl.ds(j, height * TROWS, stride=across), :]
    for ref, row in ((ra_ref, row_a), (rb_ref, row_b)):
        i = jnp.where(row == 0, 0, height - 1)
        ref[...] = out_ref[pl.ds(pl.multiple_of(i * TROWS * across, 8), TROWS * across), :]


def product_kernel(height, across, codes_ref, meta_ref, hl_ref, pairs_ref, pa_ref, pb_ref, sa_ref, sb_ref,
                   out_ref, w_ref, rep_ref):
    wide = across + 2
    row_a, row_b, col_a, col_b = halo_slots(meta_ref, height, across)
    picks = lane_iota(8) // 16 == row_iota(8)

    def spread(rows):
        parts = []
        for row in rows:
            x = jnp.where(picks, row, 0.0)
            for shift in (16, 32, 64):
                x = x + roll(x, shift)
            parts.append(x)
        return jnp.concatenate(parts, axis=0)

    def own(i, carry):
        for j in range(across):
            put_weights(
                pairs_ref[pl.ds((i * across + j) * PAIRS, PAIRS), :],
                rep_ref.at[j], w_ref, (i + 1) * wide + j + 1, NC,
            )
        for s, (ref, col) in enumerate(((pa_ref, col_a), (pb_ref, col_b))):
            rows = spread([ref[pl.ds(i * TROWS + q, 1), :] for q in range(TROWS)])
            put_weights(rows, rep_ref.at[s], w_ref, (i + 1) * wide + col, NC)
        return carry

    lax.fori_loop(0, height, own, 0)
    for s, (ref, row) in enumerate(((sa_ref, row_a), (sb_ref, row_b))):
        for j in range(wide):
            if j < across:
                col, rows = j + 1, [ref[q * across + j : q * across + j + 1, :] for q in range(TROWS)]
            else:
                col = col_a if j == across else col_b
                at = TROWS * j
                rows = [ref[at + q : at + q + 1, :] for q in range(TROWS)]
            put_weights(spread(rows), rep_ref.at[(s * wide + j) % across], w_ref, row * wide + col, NC)

    def body(i, carry):
        for k in range(KS):
            folded = [[] for _ in range(TROWS)]
            for j in range(across):
                b = i * across + j
                r = mm(
                    hl_ref[b, :, k * LANES : (k + 1) * LANES],
                    w_ref[neighbour(codes_ref, b, i, j, k, wide)],
                )
                x = r[:PAIRS] + r[PAIRS:]
                x = x + roll(x, 64)
                for q in range(TROWS):
                    folded[q].append(jnp.where(picks, x[q * 8 : (q + 1) * 8], 0.0))
            for q in range(TROWS):
                at = pl.multiple_of(((i * KS + k) * TROWS + q) * across, 8)
                out_ref[pl.ds(at, across), :] = fold_rows(folded[q])
        return carry

    lax.fori_loop(0, height, body, 0)


def swaps(count, first):
    pairs = [(i, i + 1) for i in range(first, count - 1, 2)]
    return pairs + [(b, a) for a, b in pairs]


def exchange(edges, rows, slab_odd, unit, height):
    pencils, slabs = lax.axis_size("pencil"), lax.axis_size("slab")
    got = [lax.ppermute(e, "pencil", swaps(pencils, s)) for s, e in enumerate(edges)]
    out = []
    for s, own in enumerate(rows):
        last = (slab_odd == 0) if s == 0 else (slab_odd == 1)
        corners = [
            jnp.where(last, g[(height - 1) * unit : height * unit], g[:unit]) for g in got
        ]
        out.append(
            lax.ppermute(jnp.concatenate([own] + corners, axis=0), "slab", swaps(slabs, s))
        )
    return got + out


def lines(x, features):
    height, across, _ = x.shape
    y = x.reshape(height, across, features // LANES, LANES).transpose(0, 2, 1, 3)
    return y.reshape(height * across * features // LANES, LANES)


def unlines(y, height, across, features):
    x = y.reshape(height, features // LANES, across, LANES).transpose(0, 2, 1, 3)
    return x.reshape(height, across, features)


def call(kernel, outs, ins, scratch=(), limit=LIMIT, specs=None):
    return pl.pallas_call(
        kernel,
        out_shape=outs,
        in_specs=specs,
        out_specs=[VM] * len(outs),
        scratch_shapes=list(scratch),
        compiler_params=pltpu.CompilerParams(vmem_limit_bytes=limit),
    )(*ins)


def sds(*shape, dtype=F32):
    return jax.ShapeDtypeStruct(shape, dtype)


def mode_table():
    centre = np.arange(BLK, dtype=np.float64) + 0.5
    q = np.cos(math.pi * centre[:, None] * np.arange(NC)[None, :] / BLK).astype(np.float32)
    return q


def shards(a_blocks, col_codes, agg_of, test_vectors):
    height, across = agg_of.shape
    slabs, pencils = lax.axis_size("slab"), lax.axis_size("pencil")
    devices = slabs * pencils
    block_rows = height * across
    capacity = 2 * block_rows // devices
    groups = devices // 2
    per_owner = block_rows // 8
    hcount = -(-capacity // 4)
    wide = across + 2
    slab_odd = lax.axis_index("slab") % 2
    pencil_odd = lax.axis_index("pencil") % 2
    meta = jnp.stack([slab_odd, pencil_odd]).astype(jnp.int32)
    codes = col_codes.reshape(block_rows * KS)
    group_agg = agg_of.reshape(groups, capacity)
    owner = (group_agg[:, 0] // per_owner).astype(jnp.int32)
    chosen = owner[None, :] == jnp.arange(devices, dtype=jnp.int32)[:, None]
    slot_ids = (
        jnp.sum(jnp.where(chosen[:, :, None], group_agg[None] % per_owner + 1, 0), axis=1) - 1
    ).astype(F32)
    ids = jnp.pad(slot_ids, ((0, 0), (NV, LANES - NV - capacity)))

    tv = lines(test_vectors, BLK * NV)
    by_row = test_vectors.reshape(height, across, VROWS, LANES)
    col_hi, col_lo = by_row[:, across - 1], by_row[:, 0]
    row_hi, row_lo = by_row[height - 1], by_row[0]
    flip = lambda odd, a, b: (jnp.where(odd == 0, a, b), jnp.where(odd == 0, b, a))
    edges = [e.reshape(height * VROWS, LANES) for e in flip(pencil_odd, col_hi, col_lo)]
    rows = [e.reshape(across * VROWS, LANES) for e in flip(slab_odd, row_hi, row_lo)]
    halo = exchange(edges, rows, slab_odd, VROWS, height)

    lane = np.arange(LANES)
    ones = jnp.asarray((lane[:, None] // 64) == (lane[None, :] // 32) % 2, BF16)
    chunk = KS * PAIRS * across
    hl, rd, v = call(
        functools.partial(prepare_kernel, height, across),
        [sds(block_rows, 2 * PAIRS, KS * LANES, dtype=BF16), sds(block_rows * PAIRS, LANES), sds(block_rows * PAIRS, LANES)],
        [meta, lines(a_blocks, KS * BLK * BLK), tv, ones],
        [pltpu.VMEM((4, chunk, LANES), F32), pltpu.SemaphoreType.DMA((4,))],
        specs=[SM, HB, VM, VM],
    )
    work = [
        pltpu.VMEM((wide * (height + 2), 2 * BLK, LANES), BF16),
        pltpu.VMEM((across, BLK, LANES), F32),
        pltpu.VMEM((across, PAIRS, LANES), F32),
    ]
    v, ea, eb, ra, rb = call(
        functools.partial(sweep_kernel, height, across),
        [sds(block_rows * PAIRS, LANES)] + [sds(height * VROWS, LANES)] * 2 + [sds(across * VROWS, LANES)] * 2,
        [codes, meta, hl, rd, v, *halo],
        work,
        specs=[SM, SM] + [VM] * 7,
    )
    halo = exchange([ea, eb], [ra, rb], slab_odd, VROWS, height)
    q = mode_table()
    q01 = np.concatenate([q[0::2].T, q[1::2].T], axis=0)
    q_hi = jnp.asarray(q01).astype(BF16)
    q_lo = (jnp.asarray(q01) - q_hi.astype(F32)).astype(BF16)
    modes = jnp.concatenate([q_hi, q_lo], axis=0)
    slot_rows = hcount * NC + 1
    v, pay = call(
        functools.partial(last_sweep_kernel, height, across, capacity),
        [sds(block_rows * PAIRS, LANES), sds(devices * slot_rows, LANES)],
        [codes, meta, owner, hl, rd, v, *halo, ids, modes],
        work + [pltpu.VMEM((block_rows * NC, LANES), F32)],
        specs=[SM, SM, SM] + [VM] * 9,
    )
    got = lax.all_to_all(
        pay.reshape(devices, slot_rows * LANES), ("slab", "pencil"), split_axis=0, concat_axis=0, tiled=True
    ).reshape(devices * slot_rows, LANES)
    ret, inv = call(
        functools.partial(solve_kernel, float(block_rows * BLK * devices), per_owner, capacity),
        [sds(devices * hcount * NC, LANES), sds(8, LANES)],
        [got],
        specs=[VM],
    )
    back = lax.all_to_all(
        ret.reshape(devices, hcount * NC * LANES), ("slab", "pencil"), split_axis=0, concat_axis=0, tiled=True
    ).reshape(devices * hcount * NC, LANES)
    relaxed, left = call(
        functools.partial(relaxed_kernel, height, across),
        [sds(block_rows * VROWS, LANES), sds(block_rows, PAIRS, LANES, dtype=BF16)],
        [v, inv],
        specs=[VM, VM],
    )
    pairs, tiles, ea, eb, ra, rb = call(
        functools.partial(tile_kernel, height, across, capacity),
        [sds(block_rows * PAIRS, LANES), sds(block_rows * TROWS, LANES)]
        + [sds(height * TROWS, LANES)] * 2 + [sds(across * TROWS, LANES)] * 2,
        [meta, owner, back, left],
        specs=[SM, SM, VM, VM],
    )
    halo = exchange([ea, eb], [ra, rb], slab_odd, TROWS, height)
    (products,) = call(
        functools.partial(product_kernel, height, across),
        [sds(block_rows * KS * TROWS, LANES)],
        [codes, meta, hl, pairs, *halo],
        work[:2],
        specs=[SM, SM] + [VM] * 6,
    )
    return (
        unlines(relaxed, height, across, BLK * NV),
        unlines(tiles, height, across, BLK * NC),
        unlines(products, height, across, KS * BLK * NC),
    )


def solution(mesh):
    in_specs = (P("slab", "pencil", None), P("slab", "pencil", None), P("slab", "pencil"), P("slab", "pencil", None))
    out_specs = (P("slab", "pencil", None),) * 3
    return jax.shard_map(shards, mesh=mesh, in_specs=in_specs, out_specs=out_specs, check_vma=False)
```

```python
import functools
import math

import jax
import jax.numpy as jnp
import numpy as np
from jax import lax
from jax.experimental import pallas as pl
from jax.experimental.pallas import tpu as pltpu
from jax.sharding import PartitionSpec as P

BLK = 64
NV = 32
NC = 8
KS = 5
ITERS = 2
OMEGA = 2.0 / 3.0
LANES = 128
F32 = jnp.float32
BF16 = jnp.bfloat16
PAIRS = BLK // 2
VROWS = BLK * NV // LANES
TROWS = BLK * NC // LANES
VM = pl.BlockSpec(memory_space=pltpu.VMEM)
SM = pl.BlockSpec(memory_space=pltpu.SMEM)
HB = pl.BlockSpec(memory_space=pltpu.HBM)
LIMIT = 16 * 1024 * 1024


def lane_iota(rows):
    return lax.broadcasted_iota(jnp.int32, (rows, LANES), 1)


def row_iota(rows):
    return lax.broadcasted_iota(jnp.int32, (rows, LANES), 0)


def roll(x, shift):
    return pltpu.roll(x, shift, 1)


def upper(x):
    return x.astype(BF16).astype(F32)


def hi_lo_lanes(x):
    return x - jnp.where(lane_iota(x.shape[0]) < 64, 0.0, upper(x))


def split(x):
    hi = x.astype(BF16)
    return jnp.concatenate([hi, (x - hi.astype(F32)).astype(BF16)], axis=0)


def rows_to_columns(rows, fold_ref, spread_ref):
    group = lane_iota(VROWS) // NV
    for s in range(4):
        spread_ref[pl.ds(s, VROWS, stride=4), :] = jnp.where(group == s, rows, 0.0)
    x = mm_t(fold_ref[...], split(spread_ref[...]))
    return x + roll(x, 64)


def pack_columns(x):
    return jnp.where(lane_iota(VROWS) < 64, x[:VROWS], x[VROWS:])


def unpack_columns(x):
    low = lane_iota(VROWS) < 64
    turned = roll(x, 64)
    return jnp.concatenate([jnp.where(low, x, turned), jnp.where(low, turned, x)], axis=0)


def mm_t(a, b):
    return lax.dot_general(a, b, (((1,), (1,)), ((), ())), preferred_element_type=F32)


def mm(a, b):
    return jnp.dot(a, b, preferred_element_type=F32)


def fold_rows(parts):
    sub = row_iota(8)
    step = 4
    while len(parts) > 1:
        half = len(parts) // 2
        parts = [
            jnp.where(
                (sub & step) == 0,
                parts[u] + pltpu.roll(parts[u], 8 - step, 0),
                parts[u + half] + pltpu.roll(parts[u + half], step, 0),
            )
            for u in range(half)
        ]
        step //= 2
    return parts[0]


def neighbour(near_ref, b, i, j, k, wide):
    return (i + 1) * wide + j + 1 if k == 0 else near_ref[b * KS + k]


def prepare_kernel(height, across, ints_ref, a_hbm, tv_ref, fold_ref, sent_a, sent_b, at_ref, rd_ref, v_ref, buf, rep_ref, sem):
    tiles = KS * PAIRS
    chunk = tiles * across
    depth = buf.shape[0]

    def copy(i):
        slot = lax.rem(i, depth)
        return pltpu.make_async_copy(
            a_hbm.at[pl.ds(i * chunk, chunk), :], buf.at[slot], sem.at[slot]
        )

    for i in range(depth - 1):
        copy(i).start()
    low = lane_iota(PAIRS) < 64
    row = row_iota(BLK)
    on_diagonal = lane_iota(BLK) == 2 * (row & (PAIRS - 1)) + row // PAIRS

    def body(i, carry):
        @pl.when(i + depth - 1 < height)
        def _():
            copy(i + depth - 1).start()

        copy(i).wait()
        slot = lax.rem(i, depth)
        for j in range(across):
            b = i * across + j

            def part(k):
                return buf[slot, pl.ds(k * PAIRS * across + j, PAIRS, stride=across), :]

            for t in range(3):
                x = part(2 * t)
                y = part(2 * t + 1) if t < 2 else jnp.zeros((PAIRS, LANES), F32)
                y_turned = roll(y, 64) if t < 2 else y
                m = jnp.concatenate(
                    [jnp.where(low, x, y_turned), jnp.where(low, roll(x, 64), y)], axis=0
                )
                at_ref[b, :, t * LANES : (t + 1) * LANES] = split(m)
                if t == 0:
                    d = jnp.sum(jnp.where(on_diagonal, m, 0.0), axis=0, keepdims=True)
                    rd_ref[pl.ds(b, 1), :] = OMEGA / (d + roll(d, 64))
            v_ref[pl.ds(b * NV, NV), :] = rows_to_columns(
                tv_ref[pl.ds(i * VROWS * across + j, VROWS, stride=across), :],
                fold_ref, rep_ref.at[j],
            )
        return carry

    lax.fori_loop(0, height, body, 0, unroll=2)


def halo_slots(meta_ref, height, across):
    slab_odd, pencil_odd = meta_ref[0], meta_ref[1]
    col_a = jnp.where(pencil_odd == 0, across + 1, 0)
    row_a = jnp.where(slab_odd == 0, height + 1, 0)
    return row_a, height + 1 - row_a, col_a, across + 1 - col_a


def sweep_core(height, across, near_ref, meta_ref, at_ref, rd_ref, v_ref, halo, u_ref, convert, store):
    wide = across + 2
    pa_ref, pb_ref, sa_ref, sb_ref = halo
    row_a, row_b, col_a, col_b = halo_slots(meta_ref, height, across)

    def own(i, carry):
        for j in range(across):
            u_ref[(i + 1) * wide + j + 1] = split(v_ref[pl.ds((i * across + j) * NV, NV), :])
        for s, (ref, col) in enumerate(((pa_ref, col_a), (pb_ref, col_b))):
            u_ref[(i + 1) * wide + col] = split(convert(ref[pl.ds(i * VROWS, VROWS), :], s))
        return carry

    lax.fori_loop(0, height, own, 0)
    for s, (ref, row) in enumerate(((sa_ref, row_a), (sb_ref, row_b))):
        for j in range(wide):
            col = j + 1 if j < across else (col_a if j == across else col_b)
            u_ref[row * wide + col] = split(
                convert(ref[j * VROWS : (j + 1) * VROWS, :], (s * wide + j) % across)
            )
    low = lane_iota(2 * NV) < 64
    cell = lane_iota(NV) & (BLK - 1)
    stored = (cell & 1) * PAIRS + cell // 2

    def body(i, carry):
        for j in range(across):
            b = i * across + j
            u = [u_ref[neighbour(near_ref, b, i, j, k, wide)] for k in range(KS)]
            left = jnp.concatenate(
                [jnp.where(low, u[0], u[1]), jnp.where(low, u[2], u[3]), u[4]], axis=1
            )
            r = mm_t(left, at_ref[b])
            s = r[:NV] + r[NV:]
            s = jnp.take_along_axis(s + roll(s, 64), stored, axis=1)
            store(i, j, b, v_ref[pl.ds(b * NV, NV), :] - s * rd_ref[pl.ds(b, 1), :])
        return carry

    lax.fori_loop(0, height, body, 0, unroll=2)


def sweep_kernel(height, across, near_ref, meta_ref, at_ref, rd_ref, v_ref, pa, pb, sa, sb, fold_ref,
                 out_ref, ea_ref, eb_ref, ra_ref, rb_ref, u_ref, rep_ref):
    def convert(rows, slot):
        return rows_to_columns(rows, fold_ref, rep_ref.at[slot])

    def store(i, j, b, value):
        out_ref[pl.ds(b * NV, NV), :] = value

    sweep_core(height, across, near_ref, meta_ref, at_ref, rd_ref, v_ref, (pa, pb, sa, sb),
               u_ref, convert, store)
    row_a, row_b, col_a, col_b = halo_slots(meta_ref, height, across)

    def message(i, j):
        return pack_columns(out_ref[pl.ds((i * across + j) * NV, NV), :])

    def edge(i, carry):
        for ref, col in ((ea_ref, col_a), (eb_ref, col_b)):
            ref[pl.ds(i * VROWS, VROWS), :] = message(i, jnp.where(col == 0, 0, across - 1))
        return carry

    lax.fori_loop(0, height, edge, 0)
    for ref, row in ((ra_ref, row_a), (rb_ref, row_b)):
        i = jnp.where(row == 0, 0, height - 1)
        for j in range(across):
            ref[j * VROWS : (j + 1) * VROWS, :] = message(i, j)


def last_sweep_kernel(height, across, capacity, per_owner, near_ref, meta_ref, agg_ref, at_ref, rd_ref, v_ref,
                      pa, pb, sa, sb, modes_ref, out_ref, pay_ref, u_ref):
    hcount = -(-capacity // 4)
    slot_rows = hcount * NC + 1
    devices = pay_ref.shape[0] // slot_rows

    def store(i, j, b, value):
        out_ref[pl.ds(b * NV, NV), :] = value

    sweep_core(height, across, near_ref, meta_ref, at_ref, rd_ref, v_ref, (pa, pb, sa, sb),
               u_ref, lambda rows, slot: unpack_columns(rows), store)
    pay_ref[...] = jnp.zeros(pay_ref.shape, F32)

    def coefs(i, acc):
        values = [out_ref[pl.ds((i * across + j) * NV, NV), :] for j in range(across)]
        for v in values:
            acc = acc + v * v
        for g in range(across // capacity):
            owner = lax.div(agg_ref[i * across + g * capacity], per_owner)
            for h in range(hcount):
                upper_rows, lower_rows = [], []
                for s in range(4):
                    if h * 4 + s < capacity:
                        both = split(values[g * capacity + h * 4 + s])
                    else:
                        both = jnp.zeros((2 * NV, LANES), BF16)
                    upper_rows.append(both[:NV])
                    lower_rows.append(both[NV:])
                r = mm_t(modes_ref[...], jnp.concatenate(upper_rows + lower_rows, axis=0))
                pay_ref[pl.ds(owner * slot_rows + h * NC, NC), :] = r[:NC, :LANES] + r[:NC, LANES:]
        return acc

    acc = lax.fori_loop(0, height, coefs, jnp.zeros((NV, LANES), F32))
    square = jnp.concatenate([acc, jnp.zeros((LANES - NV, LANES), F32)], axis=0)
    total = 0.5 * jnp.sum(jnp.transpose(square), axis=0, keepdims=True)
    pay_ref[pl.ds(slot_rows - 1, devices, stride=slot_rows), :] = jnp.where(
        lane_iota(devices) < NV, total, -1.0
    )
    lane = lane_iota(1)

    def mark(g, carry):
        owner = lax.div(agg_ref[g * capacity], per_owner)
        row = jnp.where(lane < NV, total, -1.0)
        for s in range(capacity):
            local = agg_ref[g * capacity + s] - owner * per_owner
            row = jnp.where(lane == NV + s, local.astype(F32), row)
        pay_ref[pl.ds(owner * slot_rows + slot_rows - 1, 1), :] = row
        return carry

    lax.fori_loop(0, height * across // capacity, mark, 0)


def solve_kernel(cells, per_owner, capacity, got_ref, ret_ref, inv_ref):
    hcount = -(-capacity // 4)
    slot_rows = hcount * NC + 1
    devices = got_ref.shape[0] // slot_rows
    lane = lane_iota(devices)
    extra = got_ref[pl.ds(slot_rows - 1, devices, stride=slot_rows), :]
    total = jnp.sum(jnp.where(lane < NV, extra, 0.0), axis=0, keepdims=True)
    total = jnp.broadcast_to(total, (8, LANES))
    total = total + roll(total, NV)
    total = total + roll(total, 64)
    inv = 1.0 / jnp.sqrt(total / cells + 1e-06)
    inv_ref[...] = jnp.transpose(jnp.broadcast_to(inv[0:1], (LANES, LANES)))[:NV]
    width = 4 * per_owner
    inner = lane & (width - 1)
    hot = []
    for h in range(hcount):
        want = jnp.full((devices, LANES), -1.0, F32)
        for s in range(min(4, capacity - 4 * h)):
            column = extra[:, NV + 4 * h + s : NV + 4 * h + s + 1]
            want = jnp.where(inner // per_owner == s, column, want)
        same = want == (inner & (per_owner - 1)).astype(F32)
        hot.append(jnp.where(same & (lane < 2 * width), 1.0, 0.0))
    hot = jnp.concatenate(hot, axis=0)
    hot_t = jnp.transpose(hot)[:width]
    parts = [
        jnp.concatenate(
            [got_ref[pl.ds(h * NC + m, devices, stride=slot_rows), :] for h in range(hcount)], axis=0
        )
        for m in range(NC)
    ]
    data = jnp.concatenate(parts, axis=1)
    ones = jnp.ones((hcount * devices, LANES), F32)
    high = jnp.concatenate([data, ones], axis=1).astype(BF16)
    rest = jnp.concatenate([data - upper(data), jnp.zeros_like(ones)], axis=1).astype(BF16)
    hot_b = hot_t.astype(BF16)
    sums = mm(hot_b, high) + mm(hot_b, rest)
    group_lane = lane_iota(per_owner) // NV

    def block(s, m):
        return sums[s * per_owner : (s + 1) * per_owner, m * LANES : (m + 1) * LANES]

    count = sum(block(s, NC) for s in range(4))
    weight = inv[0:1] / jnp.maximum(count, 1.0)
    coarse = []
    for m in range(NC):
        c = jnp.zeros((per_owner, LANES), F32)
        for s in range(4):
            c = jnp.where(group_lane == s, block(s, m), c)
        c = c + roll(c, NV)
        c = c + roll(c, 64)
        coarse.append(c * weight)

    def dot_all(x):
        for shift in (16, 8, 4, 2, 1):
            x = x + roll(x, shift)
        return x

    gram = {(a, c): dot_all(coarse[a] * coarse[c]) for a in range(NC) for c in range(a + 1)}
    ridge = 0.1 * sum(gram[m, m] for m in range(NC)) / NC + 1e-06
    for m in range(NC):
        gram[m, m] = gram[m, m] + ridge
    recip = []
    for m in range(NC):
        root = 1.0 / jnp.sqrt(gram[m, m])
        recip.append(root)
        for a in range(m + 1, NC):
            gram[a, m] = gram[a, m] * root
        for a in range(m + 1, NC):
            for c in range(m + 1, a + 1):
                gram[a, c] = gram[a, c] - gram[a, m] * gram[c, m]
    solved = list(coarse)
    for m in range(NC):
        solved[m] = solved[m] * recip[m]
        for a in range(m + 1, NC):
            solved[a] = solved[a] - gram[a, m] * solved[m]
    for m in reversed(range(NC)):
        solved[m] = solved[m] * recip[m]
        for a in range(m):
            solved[a] = solved[a] - gram[m, a] * solved[m]
    table = jnp.concatenate(
        [
            jnp.concatenate([jnp.where(group_lane == s, solved[m], 0.0) for s in range(4)], axis=0)
            for m in range(NC)
        ],
        axis=1,
    )
    stacked = jnp.concatenate([table.astype(BF16), (table - upper(table)).astype(BF16)], axis=0)
    back = mm(hot[:, : 2 * width].astype(BF16), stacked)
    for h in range(hcount):
        for m in range(NC):
            ret_ref[pl.ds(h * NC + m, devices, stride=hcount * NC), :] = back[
                h * devices : (h + 1) * devices, m * LANES : (m + 1) * LANES
            ]


def relaxed_kernel(height, across, v_ref, inv_ref, order_ref, after_ref, rel_ref):
    inv = inv_ref[...]
    group = lane_iota(VROWS) // NV

    def body(i, carry):
        for j in range(across):
            both = split(v_ref[pl.ds((i * across + j) * NV, NV), :] * inv)
            r = mm_t(order_ref[...], jnp.concatenate([both, both], axis=0))
            r = r + roll(r, NV)
            rows = r[:VROWS]
            for s in range(1, 4):
                rows = jnp.where(group == s, r[s * VROWS : (s + 1) * VROWS], rows)
            rel_ref[pl.ds(i * VROWS * across + j, VROWS, stride=across), :] = rows
        return carry

    lax.fori_loop(0, height, body, 0, unroll=2)


def cell_rows(parts, place_ref):
    left = jnp.concatenate([hi_lo_lanes(x) for part in parts for x in part], axis=0).astype(BF16)
    r = mm(left, place_ref[...])
    picks = (lane_iota(8) & (NC - 1)) == row_iota(8)
    out = []
    for n in range(len(parts)):
        for q in range(TROWS):
            out.append(
                fold_rows(
                    [
                        jnp.where(
                            picks,
                            r[(n * 8 + u) * 8 : (n * 8 + u + 1) * 8, q * LANES : (q + 1) * LANES],
                            0.0,
                        )
                        for u in range(8)
                    ]
                )
            )
    return out


def tile_kernel(height, across, capacity, per_owner, meta_ref, agg_ref, ret_ref, v_ref, inv_ref, place_ref,
                tile_ref, out_ref, ea_ref, eb_ref, ra_ref, rb_ref):
    hcount = -(-capacity // 4)
    group_lane = lane_iota(NC) // NV
    inv = inv_ref[...]

    def body(i, carry):
        tiles = []
        for g in range(across // capacity):
            owner = lax.div(agg_ref[i * across + g * capacity], per_owner)
            for h in range(hcount):
                m = ret_ref[pl.ds(pl.multiple_of((owner * hcount + h) * NC, NC), NC), :]
                m_hi = upper(m)
                left = jnp.concatenate(
                    [jnp.where(group_lane == s, x, 0.0) for x in (m_hi, m - m_hi) for s in range(4)],
                    axis=0,
                ).astype(BF16)
                upper_rows, lower_rows = [], []
                for s in range(4):
                    if h * 4 + s < capacity:
                        b = i * across + g * capacity + h * 4 + s
                        both = split(v_ref[pl.ds(b * NV, NV), :] * inv)
                    else:
                        both = jnp.zeros((2 * NV, LANES), BF16)
                    upper_rows.append(both[:NV])
                    lower_rows.append(both[NV:])
                r = mm(
                    jnp.concatenate([left, left], axis=1),
                    jnp.concatenate(upper_rows + lower_rows, axis=0),
                )
                for s in range(min(4, capacity - h * 4)):
                    t = r[s * NC : (s + 1) * NC] + r[(4 + s) * NC : (5 + s) * NC]
                    b = i * across + g * capacity + h * 4 + s
                    tile_ref[pl.ds(b * NC, NC), :] = t
                    tiles.append(t)
        for q, rows in enumerate(cell_rows([tiles], place_ref)):
            out_ref[pl.ds((i * TROWS + q) * across, across), :] = rows
        return carry

    lax.fori_loop(0, height, body, 0, unroll=2)
    row_a, row_b, col_a, col_b = halo_slots(meta_ref, height, across)

    def edge(i, carry):
        for ref, col in ((ea_ref, col_a), (eb_ref, col_b)):
            j = jnp.where(col == 0, 0, across - 1)
            ref[pl.ds(i * NC, NC), :] = tile_ref[pl.ds((i * across + j) * NC, NC), :]
        return carry

    lax.fori_loop(0, height, edge, 0)
    for ref, row in ((ra_ref, row_a), (rb_ref, row_b)):
        i = jnp.where(row == 0, 0, height - 1)
        ref[...] = tile_ref[pl.ds(pl.multiple_of(i * across * NC, 8), across * NC), :]


def product_kernel(height, across, near_ref, meta_ref, at_ref, tile_ref, pa_ref, pb_ref, sa_ref, sb_ref,
                   place_ref, out_ref, u_ref):
    wide = across + 2
    row_a, row_b, col_a, col_b = halo_slots(meta_ref, height, across)
    low = lane_iota(NC) < 64

    def put(index, x):
        hi = upper(x)
        lo = x - hi
        u_ref[index] = jnp.concatenate(
            [
                jnp.where(low, hi, 0.0), jnp.where(low, lo, 0.0),
                jnp.where(low, 0.0, hi), jnp.where(low, 0.0, lo),
            ],
            axis=0,
        ).astype(BF16)

    def own(i, carry):
        for j in range(across):
            put((i + 1) * wide + j + 1, tile_ref[pl.ds((i * across + j) * NC, NC), :])
        for ref, col in ((pa_ref, col_a), (pb_ref, col_b)):
            put((i + 1) * wide + col, ref[pl.ds(i * NC, NC), :])
        return carry

    lax.fori_loop(0, height, own, 0)
    for ref, row in ((sa_ref, row_a), (sb_ref, row_b)):
        for j in range(wide):
            col = j + 1 if j < across else (col_a if j == across else col_b)
            put(row * wide + col, ref[j * NC : (j + 1) * NC, :])

    def body(i, carry):
        parts = [[] for _ in range(KS)]
        for j in range(across):
            b = i * across + j
            u = [
                u_ref[neighbour(near_ref, b, i, j, k, wide), (k % 2) * 2 * NC : (k % 2 + 1) * 2 * NC, :]
                for k in range(KS)
            ]
            for t in range(3):
                left = jnp.concatenate(u[2 * t : 2 * t + 2], axis=0)
                r = mm_t(left, at_ref[b, :, t * LANES : (t + 1) * LANES])
                for s in range(left.shape[0] // (2 * NC)):
                    x = r[s * 2 * NC : s * 2 * NC + NC] + r[s * 2 * NC + NC : (s + 1) * 2 * NC]
                    parts[2 * t + s].append(x + roll(x, 64))
        for n, rows in enumerate(cell_rows(parts, place_ref)):
            at = pl.multiple_of((i * KS * TROWS + n) * across, 8)
            out_ref[pl.ds(at, across), :] = rows
        return carry

    lax.fori_loop(0, height, body, 0, unroll=2)


def swaps(count, first):
    pairs = [(i, i + 1) for i in range(first, count - 1, 2)]
    return pairs + [(b, a) for a, b in pairs]


def exchange(edges, rows, slab_odd, unit, height, sent=None):
    pencils, slabs = lax.axis_size("pencil"), lax.axis_size("slab")
    got = [lax.ppermute(e, "pencil", swaps(pencils, s)) for s, e in enumerate(edges)]
    out = []
    for s, own in enumerate(rows):
        last = (slab_odd == 0) if s == 0 else (slab_odd == 1)
        corners = [
            jnp.where(last, g[(height - 1) * unit : height * unit], g[:unit]) for g in got
        ]
        message = jnp.concatenate([own] + corners, axis=0)
        if sent is not None:
            sent.append(message)
        out.append(lax.ppermute(message, "slab", swaps(slabs, s)))
    return got + out


def lines(x, features):
    height, across, _ = x.shape
    y = x.reshape(height, across, features // LANES, LANES).transpose(0, 2, 1, 3)
    return y.reshape(height * across * features // LANES, LANES)


def unlines(y, height, across, features):
    x = y.reshape(height, features // LANES, across, LANES).transpose(0, 2, 1, 3)
    return x.reshape(height, across, features)


def call(kernel, outs, ins, scratch=(), limit=LIMIT, specs=None):
    return pl.pallas_call(
        kernel,
        out_shape=outs,
        in_specs=specs,
        out_specs=[VM] * len(outs),
        scratch_shapes=list(scratch),
        compiler_params=pltpu.CompilerParams(vmem_limit_bytes=limit),
    )(*ins)


def sds(*shape, dtype=F32):
    return jax.ShapeDtypeStruct(shape, dtype)


def mode_table():
    centre = np.arange(BLK, dtype=np.float64) + 0.5
    q = np.cos(math.pi * centre[:, None] * np.arange(NC)[None, :] / BLK).astype(np.float32)
    return q


def shards(a_blocks, col_codes, agg_of, test_vectors):
    height, across = agg_of.shape
    slabs, pencils = lax.axis_size("slab"), lax.axis_size("pencil")
    devices = slabs * pencils
    block_rows = height * across
    capacity = 2 * block_rows // devices
    per_owner = block_rows // 8
    hcount = -(-capacity // 4)
    wide = across + 2
    slab_odd = lax.axis_index("slab") % 2
    pencil_odd = lax.axis_index("pencil") % 2
    meta = jnp.stack([slab_odd, pencil_odd]).astype(jnp.int32)
    down = jnp.arange(height, dtype=jnp.int32)[:, None, None] + col_codes // 3
    near = (down * wide + jnp.arange(across, dtype=jnp.int32)[None, :, None] + col_codes % 3).reshape(-1)
    aggs = agg_of.reshape(-1)

    tv = lines(test_vectors, BLK * NV)
    by_row = test_vectors.reshape(height, across, VROWS, LANES)
    col_hi, col_lo = by_row[:, across - 1], by_row[:, 0]
    row_hi, row_lo = by_row[height - 1], by_row[0]
    flip = lambda odd, a, b: (jnp.where(odd == 0, a, b), jnp.where(odd == 0, b, a))
    edges = [e.reshape(height * VROWS, LANES) for e in flip(pencil_odd, col_hi, col_lo)]
    rows = [e.reshape(across * VROWS, LANES) for e in flip(slab_odd, row_hi, row_lo)]
    sent = []
    halo = exchange(edges, rows, slab_odd, VROWS, height, sent)

    lane = np.arange(LANES)
    fold = jnp.asarray(np.arange(NV)[:, None] == lane[None, :] % NV, BF16)
    place_to = np.arange(TROWS * LANES) // NC
    place = jnp.asarray((lane[:, None] % BLK) == place_to[None, :], BF16)
    stored = 2 * (lane % PAIRS) + lane % BLK // PAIRS
    place_stored = jnp.asarray(stored[:, None] == place_to[None, :], BF16)
    order_row = np.arange(BLK)
    order = jnp.asarray(((order_row % VROWS) * 4 + order_row // VROWS)[:, None] == lane[None, :], BF16)
    q = mode_table()
    q_hi = jnp.asarray(q.T).astype(BF16)
    q_lo = (jnp.asarray(q.T) - q_hi.astype(F32)).astype(BF16)
    modes = jnp.pad(jnp.concatenate([q_hi, q_lo], axis=1), ((0, NC), (0, 0)))

    chunk = KS * PAIRS * across
    ints = jnp.concatenate([near, aggs, meta])
    at, rd, v = call(
        functools.partial(prepare_kernel, height, across),
        [sds(block_rows, 2 * BLK, 3 * LANES, dtype=BF16), sds(block_rows, LANES), sds(block_rows * NV, LANES)],
        [ints, pltpu.with_memory_space_constraint(lines(a_blocks, KS * BLK * BLK), pltpu.HBM), tv, fold, *sent],
        [
            pltpu.VMEM((4, chunk, LANES), F32),
            pltpu.VMEM((across, BLK, LANES), F32),
            pltpu.SemaphoreType.DMA((4,)),
        ],
        specs=[SM, HB, VM, VM, HB, HB],
        limit=16 * 1024 * 1024,
    )
    field = [pltpu.VMEM((wide * (height + 2), 2 * NV, LANES), BF16)]
    v, ea, eb, ra, rb = call(
        functools.partial(sweep_kernel, height, across),
        [sds(block_rows * NV, LANES)] + [sds(height * VROWS, LANES)] * 2 + [sds(across * VROWS, LANES)] * 2,
        [near, meta, at, rd, v, *halo, fold],
        field + [pltpu.VMEM((across, BLK, LANES), F32)],
        specs=[SM, SM] + [VM] * 8,
    )
    halo = exchange([ea, eb], [ra, rb], slab_odd, VROWS, height)
    slot_rows = hcount * NC + 1
    v, pay = call(
        functools.partial(last_sweep_kernel, height, across, capacity, per_owner),
        [sds(block_rows * NV, LANES), sds(devices * slot_rows, LANES)],
        [near, meta, aggs, at, rd, v, *halo, modes],
        field,
        specs=[SM, SM, SM] + [VM] * 8,
    )
    got = lax.all_to_all(
        pay.reshape(devices, slot_rows * LANES), ("slab", "pencil"), split_axis=0, concat_axis=0, tiled=True
    ).reshape(devices * slot_rows, LANES)
    ret, inv = call(
        functools.partial(solve_kernel, float(block_rows * BLK * devices), per_owner, capacity),
        [sds(devices * hcount * NC, LANES), sds(NV, LANES)],
        [got],
        specs=[VM],
    )
    back = lax.all_to_all(
        ret.reshape(devices, hcount * NC * LANES), ("slab", "pencil"), split_axis=0, concat_axis=0, tiled=True
    ).reshape(devices * hcount * NC, LANES)
    tile, tiles, ea, eb, ra, rb = call(
        functools.partial(tile_kernel, height, across, capacity, per_owner),
        [sds(block_rows * NC, LANES), sds(block_rows * TROWS, LANES)]
        + [sds(height * NC, LANES)] * 2 + [sds(across * NC, LANES)] * 2,
        [meta, aggs, back, v, inv, place],
        specs=[SM, SM, VM, VM, VM, VM],
    )
    (relaxed,) = call(
        functools.partial(relaxed_kernel, height, across),
        [sds(block_rows * VROWS, LANES)],
        [v, inv, order, tile],
        specs=[VM] * 4,
    )
    halo = exchange([ea, eb], [ra, rb], slab_odd, NC, height)
    (products,) = call(
        functools.partial(product_kernel, height, across),
        [sds(block_rows * KS * TROWS, LANES)],
        [near, meta, at, tile, *halo, place_stored],
        [pltpu.VMEM((wide * (height + 2), 4 * NC, LANES), BF16)],
        specs=[SM, SM] + [VM] * 7,
    )
    return (
        unlines(relaxed, height, across, BLK * NV),
        unlines(tiles, height, across, BLK * NC),
        unlines(products, height, across, KS * BLK * NC),
    )


def solution(mesh):
    in_specs = (P("slab", "pencil", None), P("slab", "pencil", None), P("slab", "pencil"), P("slab", "pencil", None))
    out_specs = (P("slab", "pencil", None),) * 3
    return jax.shard_map(shards, mesh=mesh, in_specs=in_specs, out_specs=out_specs, check_vma=False)
```

```python
import functools
import math

import jax
import jax.numpy as jnp
import numpy as np
from jax import lax
from jax.experimental import pallas as pl
from jax.experimental.pallas import tpu as pltpu
from jax.sharding import PartitionSpec as P

BLK = 64
NV = 32
NC = 8
KS = 5
ITERS = 2
OMEGA = 2.0 / 3.0
LANES = 128
F32 = jnp.float32
BF16 = jnp.bfloat16
PAIRS = BLK // 2
VROWS = BLK * NV // LANES
TROWS = BLK * NC // LANES
VM = pl.BlockSpec(memory_space=pltpu.VMEM)
SM = pl.BlockSpec(memory_space=pltpu.SMEM)
HB = pl.BlockSpec(memory_space=pltpu.HBM)
LIMIT = 16 * 1024 * 1024


def lane_iota(rows):
    return lax.broadcasted_iota(jnp.int32, (rows, LANES), 1)


def row_iota(rows):
    return lax.broadcasted_iota(jnp.int32, (rows, LANES), 0)


def roll(x, shift):
    return pltpu.roll(x, shift, 1)


def upper(x):
    return x.astype(BF16).astype(F32)


def hi_lo_lanes(x):
    return x - jnp.where(lane_iota(x.shape[0]) < 64, 0.0, upper(x))


def split(x):
    hi = x.astype(BF16)
    return jnp.concatenate([hi, (x - hi.astype(F32)).astype(BF16)], axis=0)


def rows_to_columns(rows, fold_ref, spread_ref):
    group = lane_iota(VROWS) // NV
    for s in range(4):
        spread_ref[pl.ds(s, VROWS, stride=4), :] = jnp.where(group == s, rows, 0.0)
    x = mm_t(fold_ref[...], split(spread_ref[...]))
    return x + roll(x, 64)


def pack_columns(x):
    return jnp.where(lane_iota(VROWS) < 64, x[:VROWS], x[VROWS:])


def unpack_columns(x):
    low = lane_iota(VROWS) < 64
    turned = roll(x, 64)
    return jnp.concatenate([jnp.where(low, x, turned), jnp.where(low, turned, x)], axis=0)


def mm_t(a, b):
    return lax.dot_general(a, b, (((1,), (1,)), ((), ())), preferred_element_type=F32)


def mm(a, b):
    return jnp.dot(a, b, preferred_element_type=F32)


def fold_rows(parts):
    sub = row_iota(8)
    step = 4
    while len(parts) > 1:
        half = len(parts) // 2
        parts = [
            jnp.where(
                (sub & step) == 0,
                parts[u] + pltpu.roll(parts[u], 8 - step, 0),
                parts[u + half] + pltpu.roll(parts[u + half], step, 0),
            )
            for u in range(half)
        ]
        step //= 2
    return parts[0]


def neighbour(near_ref, b, i, j, k, wide):
    return (i + 1) * wide + j + 1 if k == 0 else near_ref[b * KS + k]


def prepare_kernel(height, across, ints_ref, a_hbm, tv_ref, fold_ref, turn_ref, sent_a, sent_b, at_ref, rd_ref, v_ref, buf, rep_ref, sem):
    tiles = KS * PAIRS
    chunk = tiles * across
    depth = buf.shape[0]

    def copy(i):
        slot = lax.rem(i, depth)
        return pltpu.make_async_copy(
            a_hbm.at[pl.ds(i * chunk, chunk), :], buf.at[slot], sem.at[slot]
        )

    for i in range(depth - 1):
        copy(i).start()
    low = lane_iota(2 * PAIRS) < 64
    lane = lane_iota(PAIRS)
    on_diagonal = (lane & (BLK - 1)) == 2 * row_iota(PAIRS) + lane // BLK

    def body(i, carry):
        @pl.when(i + depth - 1 < height)
        def _():
            copy(i + depth - 1).start()

        copy(i).wait()
        slot = lax.rem(i, depth)
        for j in range(across):
            b = i * across + j

            def part(k):
                return buf[slot, pl.ds(k * PAIRS * across + j, PAIRS, stride=across), :]

            for first, slots in ((0, 2), (2, 2), (4, 1)):
                halves = []
                for k in range(first, first + slots):
                    x = part(k)
                    if k == 0:
                        d = jnp.sum(jnp.where(on_diagonal, x, 0.0), axis=0, keepdims=True)
                        rd_ref[pl.ds(b, 1), :] = OMEGA / (d + roll(d, 64))
                    m = split(x)
                    zero = jnp.zeros_like(m)
                    halves += [jnp.where(low, m, zero), jnp.where(low, zero, m)]
                y = mm_t(turn_ref[...], jnp.concatenate(halves, axis=0)).astype(BF16)
                for u in range(slots):
                    k = first + u
                    at_ref[b, k * BLK : (k + 1) * BLK, :] = y[:, u * LANES : (u + 1) * LANES]
            v_ref[pl.ds(b * NV, NV), :] = rows_to_columns(
                tv_ref[pl.ds(i * VROWS * across + j, VROWS, stride=across), :],
                fold_ref, rep_ref.at[j],
            )
        return carry

    lax.fori_loop(0, height, body, 0, unroll=2)


def halo_slots(meta_ref, height, across):
    slab_odd, pencil_odd = meta_ref[0], meta_ref[1]
    col_a = jnp.where(pencil_odd == 0, across + 1, 0)
    row_a = jnp.where(slab_odd == 0, height + 1, 0)
    return row_a, height + 1 - row_a, col_a, across + 1 - col_a


def fill_own(height, across, meta_ref, v_ref, pencil, u_ref, convert):
    wide = across + 2
    _, _, col_a, col_b = halo_slots(meta_ref, height, across)

    def own(i, carry):
        for j in range(across):
            u_ref[(i + 1) * wide + j + 1] = split(v_ref[pl.ds((i * across + j) * NV, NV), :])
        for s, (ref, col) in enumerate(zip(pencil, (col_a, col_b))):
            u_ref[(i + 1) * wide + col] = split(convert(ref[pl.ds(i * VROWS, VROWS), :], s))
        return carry

    lax.fori_loop(0, height, own, 0, unroll=2)


def fill_slab(height, across, meta_ref, slab, u_ref, convert):
    wide = across + 2
    row_a, row_b, col_a, col_b = halo_slots(meta_ref, height, across)
    for s, (ref, row) in enumerate(zip(slab, (row_a, row_b))):
        for j in range(wide):
            col = j + 1 if j < across else (col_a if j == across else col_b)
            u_ref[row * wide + col] = split(
                convert(ref[j * VROWS : (j + 1) * VROWS, :], (s * wide + j) % across)
            )


def sweep_rows(height, across, first, last, near_ref, at_ref, rd_ref, v_ref, u_ref, out_ref):
    wide = across + 2
    low = lane_iota(2 * NV) < 64
    cell = lane_iota(NV) & (BLK - 1)
    stored = (cell & 1) * BLK + cell // 2

    def body(i, carry):
        for j in range(across):
            b = i * across + j
            u = [u_ref[neighbour(near_ref, b, i, j, k, wide)] for k in range(KS)]
            left = jnp.concatenate(
                [jnp.where(low, u[0], u[1]), jnp.where(low, u[2], u[3]), u[4][:, :BLK]], axis=1
            )
            r = mm(left, at_ref[b])
            s = r[:NV] + r[NV:]
            s = jnp.take_along_axis(s, stored, axis=1) + jnp.take_along_axis(s, stored + PAIRS, axis=1)
            at = pl.ds(b * NV, NV)
            out_ref[at, :] = v_ref[at, :] - s * rd_ref[pl.ds(b, 1), :]
        return carry

    if last is None:
        for i in first:
            body(i, 0)
    else:
        lax.fori_loop(first, last, body, 0, unroll=2)


def sweep_kernel(height, across, near_ref, meta_ref, at_ref, rd_ref, v_ref, pa, pb, sa, sb, fold_ref,
                 out_ref, ea_ref, eb_ref, ra_ref, rb_ref, u_ref, rep_ref):
    def convert(rows, slot):
        return rows_to_columns(rows, fold_ref, rep_ref.at[slot])

    fill_own(height, across, meta_ref, v_ref, (pa, pb), u_ref, convert)
    fill_slab(height, across, meta_ref, (sa, sb), u_ref, convert)
    sweep_rows(height, across, 0, height, near_ref, at_ref, rd_ref, v_ref, u_ref, out_ref)
    row_a, row_b, col_a, col_b = halo_slots(meta_ref, height, across)

    def message(i, j):
        return pack_columns(out_ref[pl.ds((i * across + j) * NV, NV), :])

    def edge(i, carry):
        for ref, col in ((ea_ref, col_a), (eb_ref, col_b)):
            ref[pl.ds(i * VROWS, VROWS), :] = message(i, jnp.where(col == 0, 0, across - 1))
        return carry

    lax.fori_loop(0, height, edge, 0)
    for ref, row in ((ra_ref, row_a), (rb_ref, row_b)):
        i = jnp.where(row == 0, 0, height - 1)
        for j in range(across):
            ref[j * VROWS : (j + 1) * VROWS, :] = message(i, j)


def unpack_received(rows, slot):
    return unpack_columns(rows)


def coefficients(across, capacity, per_owner, i, acc, agg_ref, modes_ref, out_ref, pay_ref):
    hcount = -(-capacity // 4)
    slot_rows = hcount * NC + 1
    values = [out_ref[pl.ds((i * across + j) * NV, NV), :] for j in range(across)]
    for v in values:
        acc = acc + v * v
    for g in range(across // capacity):
        owner = lax.div(agg_ref[i * across + g * capacity], per_owner)
        for h in range(hcount):
            upper_rows, lower_rows = [], []
            for s in range(4):
                if h * 4 + s < capacity:
                    both = split(values[g * capacity + h * 4 + s])
                else:
                    both = jnp.zeros((2 * NV, LANES), BF16)
                upper_rows.append(both[:NV])
                lower_rows.append(both[NV:])
            r = mm_t(modes_ref[...], jnp.concatenate(upper_rows + lower_rows, axis=0))
            pay_ref[pl.ds(owner * slot_rows + h * NC, NC), :] = r[:NC, :LANES] + r[:NC, LANES:]
    return acc


def inner_sweep_kernel(height, across, capacity, per_owner, near_ref, meta_ref, agg_ref, at_ref, rd_ref, v_ref,
                       pa, pb, modes_ref, out_ref, u_ref, pay_ref, acc_ref):
    fill_own(height, across, meta_ref, v_ref, (pa, pb), u_ref, unpack_received)
    sweep_rows(height, across, 1, height - 1, near_ref, at_ref, rd_ref, v_ref, u_ref, out_ref)
    pay_ref[...] = jnp.zeros(pay_ref.shape, F32)

    def coefs(i, acc):
        return coefficients(across, capacity, per_owner, i, acc, agg_ref, modes_ref, out_ref, pay_ref)

    acc_ref[...] = lax.fori_loop(1, height - 1, coefs, jnp.zeros((NV, LANES), F32), unroll=2)


def outer_sweep_kernel(height, across, capacity, per_owner, near_ref, meta_ref, agg_ref, at_ref, rd_ref, v_ref,
                       sa, sb, modes_ref, acc_ref, out_in, u_in, pay_in, out_ref, u_ref, pay_ref):
    hcount = -(-capacity // 4)
    slot_rows = hcount * NC + 1
    devices = pay_ref.shape[0] // slot_rows
    fill_slab(height, across, meta_ref, (sa, sb), u_ref, unpack_received)
    sweep_rows(height, across, (0, height - 1), None, near_ref, at_ref, rd_ref, v_ref, u_ref, out_ref)
    acc = acc_ref[...]
    for i in (0, height - 1):
        acc = coefficients(across, capacity, per_owner, i, acc, agg_ref, modes_ref, out_ref, pay_ref)
    square = jnp.concatenate([acc, jnp.zeros((LANES - NV, LANES), F32)], axis=0)
    total = 0.5 * jnp.sum(jnp.transpose(square), axis=0, keepdims=True)
    pay_ref[pl.ds(slot_rows - 1, devices, stride=slot_rows), :] = jnp.where(
        lane_iota(devices) < NV, total, -1.0
    )
    lane = lane_iota(1)

    def mark(g, carry):
        owner = lax.div(agg_ref[g * capacity], per_owner)
        row = jnp.where(lane < NV, total, -1.0)
        for s in range(capacity):
            local = agg_ref[g * capacity + s] - owner * per_owner
            row = jnp.where(lane == NV + s, local.astype(F32), row)
        pay_ref[pl.ds(owner * slot_rows + slot_rows - 1, 1), :] = row
        return carry

    lax.fori_loop(0, height * across // capacity, mark, 0, unroll=4)


def solve_kernel(cells, per_owner, capacity, got_ref, ret_ref, inv_ref):
    hcount = -(-capacity // 4)
    slot_rows = hcount * NC + 1
    devices = got_ref.shape[0] // slot_rows
    lane = lane_iota(devices)
    extra = got_ref[pl.ds(slot_rows - 1, devices, stride=slot_rows), :]
    total = jnp.sum(jnp.where(lane < NV, extra, 0.0), axis=0, keepdims=True)
    total = jnp.broadcast_to(total, (8, LANES))
    total = total + roll(total, NV)
    total = total + roll(total, 64)
    inv = 1.0 / jnp.sqrt(total / cells + 1e-06)
    inv_ref[...] = jnp.transpose(jnp.broadcast_to(inv[0:1], (LANES, LANES)))[:NV]
    width = 4 * per_owner
    inner = lane & (width - 1)
    hot = []
    for h in range(hcount):
        want = jnp.full((devices, LANES), -1.0, F32)
        for s in range(min(4, capacity - 4 * h)):
            column = extra[:, NV + 4 * h + s : NV + 4 * h + s + 1]
            want = jnp.where(inner // per_owner == s, column, want)
        same = want == (inner & (per_owner - 1)).astype(F32)
        hot.append(jnp.where(same & (lane < 2 * width), 1.0, 0.0))
    hot = jnp.concatenate(hot, axis=0)
    hot_t = jnp.transpose(hot)[:width]
    parts = [
        jnp.concatenate(
            [got_ref[pl.ds(h * NC + m, devices, stride=slot_rows), :] for h in range(hcount)], axis=0
        )
        for m in range(NC)
    ]
    data = jnp.concatenate(parts, axis=1)
    ones = jnp.ones((hcount * devices, LANES), F32)
    high = jnp.concatenate([data, ones], axis=1).astype(BF16)
    rest = jnp.concatenate([data - upper(data), jnp.zeros_like(ones)], axis=1).astype(BF16)
    hot_b = hot_t.astype(BF16)
    sums = mm(hot_b, high) + mm(hot_b, rest)
    group_lane = lane_iota(per_owner) // NV

    def block(s, m):
        return sums[s * per_owner : (s + 1) * per_owner, m * LANES : (m + 1) * LANES]

    count = sum(block(s, NC) for s in range(4))
    weight = inv[0:1] / jnp.maximum(count, 1.0)
    coarse = []
    for m in range(NC):
        c = jnp.zeros((per_owner, LANES), F32)
        for s in range(4):
            c = jnp.where(group_lane == s, block(s, m), c)
        c = c + roll(c, NV)
        c = c + roll(c, 64)
        coarse.append(c * weight)

    def dot_all(x):
        for shift in (16, 8, 4, 2, 1):
            x = x + roll(x, shift)
        return x

    gram = {(a, c): dot_all(coarse[a] * coarse[c]) for a in range(NC) for c in range(a + 1)}
    ridge = 0.1 * sum(gram[m, m] for m in range(NC)) / NC + 1e-06
    for m in range(NC):
        gram[m, m] = gram[m, m] + ridge
    recip = []
    for m in range(NC):
        root = 1.0 / jnp.sqrt(gram[m, m])
        recip.append(root)
        for a in range(m + 1, NC):
            gram[a, m] = gram[a, m] * root
        for a in range(m + 1, NC):
            for c in range(m + 1, a + 1):
                gram[a, c] = gram[a, c] - gram[a, m] * gram[c, m]
    solved = list(coarse)
    for m in range(NC):
        solved[m] = solved[m] * recip[m]
        for a in range(m + 1, NC):
            solved[a] = solved[a] - gram[a, m] * solved[m]
    for m in reversed(range(NC)):
        solved[m] = solved[m] * recip[m]
        for a in range(m):
            solved[a] = solved[a] - gram[m, a] * solved[m]
    table = jnp.concatenate(
        [
            jnp.concatenate([jnp.where(group_lane == s, solved[m], 0.0) for s in range(4)], axis=0)
            for m in range(NC)
        ],
        axis=1,
    )
    stacked = jnp.concatenate([table.astype(BF16), (table - upper(table)).astype(BF16)], axis=0)
    back = mm(hot[:, : 2 * width].astype(BF16), stacked)
    for h in range(hcount):
        for m in range(NC):
            ret_ref[pl.ds(h * NC + m, devices, stride=hcount * NC), :] = back[
                h * devices : (h + 1) * devices, m * LANES : (m + 1) * LANES
            ]


def relaxed_kernel(height, across, v_ref, inv_ref, order_ref, after_ref, rel_ref):
    inv = inv_ref[...]
    group = lane_iota(VROWS) // NV

    def body(i, carry):
        for j in range(across):
            both = split(v_ref[pl.ds((i * across + j) * NV, NV), :] * inv)
            r = mm_t(order_ref[...], jnp.concatenate([both, both], axis=0))
            r = r + roll(r, NV)
            rows = r[:VROWS]
            for s in range(1, 4):
                rows = jnp.where(group == s, r[s * VROWS : (s + 1) * VROWS], rows)
            rel_ref[pl.ds(i * VROWS * across + j, VROWS, stride=across), :] = rows
        return carry

    lax.fori_loop(0, height, body, 0, unroll=2)


def cell_rows(parts, place_ref):
    x = jnp.concatenate([x for part in parts for x in part], axis=0)
    hi = x.astype(BF16)
    r = mm(jnp.concatenate([hi, (x - hi.astype(F32)).astype(BF16)], axis=1), place_ref[...])
    picks = (lane_iota(8) & (NC - 1)) == row_iota(8)
    out = []
    for n in range(len(parts)):
        for q in range(TROWS):
            out.append(
                fold_rows(
                    [
                        jnp.where(
                            picks,
                            r[(n * 8 + u) * 8 : (n * 8 + u + 1) * 8, q * LANES : (q + 1) * LANES],
                            0.0,
                        )
                        for u in range(8)
                    ]
                )
            )
    return out


def tile_kernel(height, across, capacity, per_owner, meta_ref, agg_ref, ret_ref, v_ref, inv_ref, place_ref,
                tile_ref, out_ref, ea_ref, eb_ref, ra_ref, rb_ref):
    hcount = -(-capacity // 4)
    group_lane = lane_iota(NC) // NV
    inv = inv_ref[...]

    def body(i, carry):
        tiles = []
        for g in range(across // capacity):
            owner = lax.div(agg_ref[i * across + g * capacity], per_owner)
            for h in range(hcount):
                m = ret_ref[pl.ds(pl.multiple_of((owner * hcount + h) * NC, NC), NC), :]
                m_hi = upper(m)
                left = jnp.concatenate(
                    [jnp.where(group_lane == s, x, 0.0) for x in (m_hi, m - m_hi) for s in range(4)],
                    axis=0,
                ).astype(BF16)
                upper_rows, lower_rows = [], []
                for s in range(4):
                    if h * 4 + s < capacity:
                        b = i * across + g * capacity + h * 4 + s
                        both = split(v_ref[pl.ds(b * NV, NV), :] * inv)
                    else:
                        both = jnp.zeros((2 * NV, LANES), BF16)
                    upper_rows.append(both[:NV])
                    lower_rows.append(both[NV:])
                r = mm(
                    jnp.concatenate([left, left], axis=1),
                    jnp.concatenate(upper_rows + lower_rows, axis=0),
                )
                for s in range(min(4, capacity - h * 4)):
                    t = r[s * NC : (s + 1) * NC] + r[(4 + s) * NC : (5 + s) * NC]
                    b = i * across + g * capacity + h * 4 + s
                    tile_ref[pl.ds(b * NC, NC), :] = t
                    tiles.append(t)
        return carry

    lax.fori_loop(0, height, body, 0, unroll=2)
    step = 4 if height % 4 == 0 else 1

    def rows(s, carry):
        parts = [
            [tile_ref[pl.ds(((s * step + i) * across + j) * NC, NC), :] for j in range(across)]
            for i in range(step)
        ]
        for n, x in enumerate(cell_rows(parts, place_ref)):
            at = pl.multiple_of((s * step * TROWS + n) * across, 8)
            out_ref[pl.ds(at, across), :] = x
        return carry

    lax.fori_loop(0, height // step, rows, 0)
    row_a, row_b, col_a, col_b = halo_slots(meta_ref, height, across)

    def edge(i, carry):
        for ref, col in ((ea_ref, col_a), (eb_ref, col_b)):
            j = jnp.where(col == 0, 0, across - 1)
            ref[pl.ds(i * NC, NC), :] = tile_ref[pl.ds((i * across + j) * NC, NC), :]
        return carry

    lax.fori_loop(0, height, edge, 0)
    for ref, row in ((ra_ref, row_a), (rb_ref, row_b)):
        i = jnp.where(row == 0, 0, height - 1)
        ref[...] = tile_ref[pl.ds(pl.multiple_of(i * across * NC, 8), across * NC), :]


def product_kernel(height, across, near_ref, meta_ref, at_ref, tile_ref, pa_ref, pb_ref, sa_ref, sb_ref,
                   place_ref, out_ref, u_ref):
    wide = across + 2
    row_a, row_b, col_a, col_b = halo_slots(meta_ref, height, across)
    low = lane_iota(NC) < 64

    def put(index, x):
        hi = upper(x)
        lo = x - hi
        u_ref[index] = jnp.concatenate(
            [
                jnp.where(low, hi, 0.0), jnp.where(low, lo, 0.0),
                jnp.where(low, 0.0, hi), jnp.where(low, 0.0, lo),
            ],
            axis=0,
        ).astype(BF16)

    def own(i, carry):
        for j in range(across):
            put((i + 1) * wide + j + 1, tile_ref[pl.ds((i * across + j) * NC, NC), :])
        for ref, col in ((pa_ref, col_a), (pb_ref, col_b)):
            put((i + 1) * wide + col, ref[pl.ds(i * NC, NC), :])
        return carry

    lax.fori_loop(0, height, own, 0)
    for ref, row in ((sa_ref, row_a), (sb_ref, row_b)):
        for j in range(wide):
            col = j + 1 if j < across else (col_a if j == across else col_b)
            put(row * wide + col, ref[j * NC : (j + 1) * NC, :])

    def body(i, carry):
        parts = [[] for _ in range(KS)]
        for j in range(across):
            b = i * across + j
            u = [
                u_ref[neighbour(near_ref, b, i, j, k, wide), (k % 2) * 2 * NC : (k % 2 + 1) * 2 * NC, :]
                for k in range(KS)
            ]
            for t in range(3):
                left = jnp.concatenate(u[2 * t : 2 * t + 2], axis=0)
                if t < 2:
                    r = mm(left, at_ref[b, t * LANES : (t + 1) * LANES, :])
                else:
                    r = mm(left[:, :BLK], at_ref[b, 2 * LANES : 2 * LANES + BLK, :])
                for s in range(left.shape[0] // (2 * NC)):
                    parts[2 * t + s].append(
                        r[s * 2 * NC : s * 2 * NC + NC] + r[s * 2 * NC + NC : (s + 1) * 2 * NC]
                    )
        for n, rows in enumerate(cell_rows(parts, place_ref)):
            at = pl.multiple_of((i * KS * TROWS + n) * across, 8)
            out_ref[pl.ds(at, across), :] = rows
        return carry

    lax.fori_loop(0, height, body, 0, unroll=2)


def swaps(count, first):
    pairs = [(i, i + 1) for i in range(first, count - 1, 2)]
    return pairs + [(b, a) for a, b in pairs]


def exchange(edges, rows, slab_odd, unit, height, sent=None):
    pencils, slabs = lax.axis_size("pencil"), lax.axis_size("slab")
    got = [lax.ppermute(e, "pencil", swaps(pencils, s)) for s, e in enumerate(edges)]
    out = []
    for s, own in enumerate(rows):
        last = (slab_odd == 0) if s == 0 else (slab_odd == 1)
        corners = [
            jnp.where(last, g[(height - 1) * unit : height * unit], g[:unit]) for g in got
        ]
        message = jnp.concatenate([own] + corners, axis=0)
        if sent is not None:
            sent.append(message)
        out.append(lax.ppermute(message, "slab", swaps(slabs, s)))
    return got + out


def lines(x, features):
    height, across, _ = x.shape
    y = x.reshape(height, across, features // LANES, LANES).transpose(0, 2, 1, 3)
    return y.reshape(height * across * features // LANES, LANES)


def unlines(y, height, across, features):
    x = y.reshape(height, features // LANES, across, LANES).transpose(0, 2, 1, 3)
    return x.reshape(height, across, features)


def call(kernel, outs, ins, scratch=(), limit=LIMIT, specs=None, aliases=None):
    return pl.pallas_call(
        kernel,
        out_shape=outs,
        in_specs=specs,
        out_specs=[VM] * len(outs),
        scratch_shapes=list(scratch),
        input_output_aliases=aliases or {},
        compiler_params=pltpu.CompilerParams(vmem_limit_bytes=limit),
    )(*ins)


def sds(*shape, dtype=F32):
    return jax.ShapeDtypeStruct(shape, dtype)


def mode_table():
    centre = np.arange(BLK, dtype=np.float64) + 0.5
    q = np.cos(math.pi * centre[:, None] * np.arange(NC)[None, :] / BLK).astype(np.float32)
    return q


def shards(a_blocks, col_codes, agg_of, test_vectors):
    height, across = agg_of.shape
    slabs, pencils = lax.axis_size("slab"), lax.axis_size("pencil")
    devices = slabs * pencils
    block_rows = height * across
    capacity = 2 * block_rows // devices
    per_owner = block_rows // 8
    hcount = -(-capacity // 4)
    wide = across + 2
    slab_odd = lax.axis_index("slab") % 2
    pencil_odd = lax.axis_index("pencil") % 2
    meta = jnp.stack([slab_odd, pencil_odd]).astype(jnp.int32)
    down = jnp.arange(height, dtype=jnp.int32)[:, None, None] + col_codes // 3
    near = (down * wide + jnp.arange(across, dtype=jnp.int32)[None, :, None] + col_codes % 3).reshape(-1)
    aggs = agg_of.reshape(-1)

    tv = lines(test_vectors, BLK * NV)
    by_row = test_vectors.reshape(height, across, VROWS, LANES)
    col_hi, col_lo = by_row[:, across - 1], by_row[:, 0]
    row_hi, row_lo = by_row[height - 1], by_row[0]
    flip = lambda odd, a, b: (jnp.where(odd == 0, a, b), jnp.where(odd == 0, b, a))
    edges = [e.reshape(height * VROWS, LANES) for e in flip(pencil_odd, col_hi, col_lo)]
    rows = [e.reshape(across * VROWS, LANES) for e in flip(slab_odd, row_hi, row_lo)]
    sent = []
    halo = exchange(edges, rows, slab_odd, VROWS, height, sent)

    lane = np.arange(LANES)
    fold = jnp.asarray(np.arange(NV)[:, None] == lane[None, :] % NV, BF16)
    place_to = np.arange(TROWS * LANES) // NC
    place_one = ((lane[:, None] % BLK) == place_to[None, :]) & (lane[:, None] < BLK)
    place = jnp.asarray(np.concatenate([place_one, place_one], axis=0), BF16)
    turn = jnp.asarray(np.arange(BLK)[:, None] == lane[None, :] % BLK, BF16)
    stored = 2 * (lane % PAIRS) + lane // BLK
    place_one = stored[:, None] == place_to[None, :]
    place_stored = jnp.asarray(np.concatenate([place_one, place_one], axis=0), BF16)
    order_row = np.arange(BLK)
    order = jnp.asarray(((order_row % VROWS) * 4 + order_row // VROWS)[:, None] == lane[None, :], BF16)
    q = mode_table()
    q_hi = jnp.asarray(q.T).astype(BF16)
    q_lo = (jnp.asarray(q.T) - q_hi.astype(F32)).astype(BF16)
    modes = jnp.pad(jnp.concatenate([q_hi, q_lo], axis=1), ((0, NC), (0, 0)))

    chunk = KS * PAIRS * across
    ints = jnp.concatenate([near, aggs, meta])
    at, rd, v = call(
        functools.partial(prepare_kernel, height, across),
        [sds(block_rows, KS * BLK, LANES, dtype=BF16), sds(block_rows, LANES), sds(block_rows * NV, LANES)],
        [ints, pltpu.with_memory_space_constraint(lines(a_blocks, KS * BLK * BLK), pltpu.HBM), tv, fold, turn, *sent],
        [
            pltpu.VMEM((4, chunk, LANES), F32),
            pltpu.VMEM((across, BLK, LANES), F32),
            pltpu.SemaphoreType.DMA((4,)),
        ],
        specs=[SM, HB, VM, VM, VM, HB, HB],
        limit=16 * 1024 * 1024,
    )
    field = [pltpu.VMEM((wide * (height + 2), 2 * NV, LANES), BF16)]
    v, ea, eb, ra, rb = call(
        functools.partial(sweep_kernel, height, across),
        [sds(block_rows * NV, LANES)] + [sds(height * VROWS, LANES)] * 2 + [sds(across * VROWS, LANES)] * 2,
        [near, meta, at, rd, v, *halo, fold],
        field + [pltpu.VMEM((across, BLK, LANES), F32)],
        specs=[SM, SM] + [VM] * 8,
    )
    halo = exchange([ea, eb], [ra, rb], slab_odd, VROWS, height)
    slot_rows = hcount * NC + 1
    outs = [
        sds(block_rows * NV, LANES),
        sds(wide * (height + 2), 2 * NV, LANES, dtype=BF16),
        sds(devices * slot_rows, LANES),
    ]
    sizes = (height, across, capacity, per_owner)
    *partial, acc = call(
        functools.partial(inner_sweep_kernel, *sizes),
        outs + [sds(NV, LANES)],
        [near, meta, aggs, at, rd, v, *halo[:2], modes],
        specs=[SM, SM, SM] + [VM] * 6,
    )
    v, _, pay = call(
        functools.partial(outer_sweep_kernel, *sizes),
        outs,
        [near, meta, aggs, at, rd, v, *halo[2:], modes, acc, *partial],
        specs=[SM, SM, SM] + [VM] * 10,
        aliases={10: 0, 11: 1, 12: 2},
    )
    got = lax.all_to_all(
        pay.reshape(devices, slot_rows * LANES), ("slab", "pencil"), split_axis=0, concat_axis=0, tiled=True
    ).reshape(devices * slot_rows, LANES)
    ret, inv = call(
        functools.partial(solve_kernel, float(block_rows * BLK * devices), per_owner, capacity),
        [sds(devices * hcount * NC, LANES), sds(NV, LANES)],
        [got],
        specs=[VM],
    )
    back = lax.all_to_all(
        ret.reshape(devices, hcount * NC * LANES), ("slab", "pencil"), split_axis=0, concat_axis=0, tiled=True
    ).reshape(devices * hcount * NC, LANES)
    tile, tiles, ea, eb, ra, rb = call(
        functools.partial(tile_kernel, height, across, capacity, per_owner),
        [sds(block_rows * NC, LANES), sds(block_rows * TROWS, LANES)]
        + [sds(height * NC, LANES)] * 2 + [sds(across * NC, LANES)] * 2,
        [meta, aggs, back, v, inv, place],
        specs=[SM, SM, VM, VM, VM, VM],
    )
    (relaxed,) = call(
        functools.partial(relaxed_kernel, height, across),
        [sds(block_rows * VROWS, LANES)],
        [v, inv, order, tile],
        specs=[VM] * 4,
    )
    halo = exchange([ea, eb], [ra, rb], slab_odd, NC, height)
    (products,) = call(
        functools.partial(product_kernel, height, across),
        [sds(block_rows * KS * TROWS, LANES)],
        [near, meta, at, tile, *halo, place_stored],
        [pltpu.VMEM((wide * (height + 2), 4 * NC, LANES), BF16)],
        specs=[SM, SM] + [VM] * 7,
    )
    return (
        unlines(relaxed, height, across, BLK * NV),
        unlines(tiles, height, across, BLK * NC),
        unlines(products, height, across, KS * BLK * NC),
    )


def solution(mesh):
    in_specs = (P("slab", "pencil", None), P("slab", "pencil", None), P("slab", "pencil"), P("slab", "pencil", None))
    out_specs = (P("slab", "pencil", None),) * 3
    return jax.shard_map(shards, mesh=mesh, in_specs=in_specs, out_specs=out_specs, check_vma=False)
```

```python
import functools
import math

import jax
import jax.numpy as jnp
import numpy as np
from jax import lax
from jax.experimental import pallas as pl
from jax.experimental.pallas import tpu as pltpu
from jax.sharding import PartitionSpec as P

BLK = 64
NV = 32
NC = 8
KS = 5
ITERS = 2
OMEGA = 2.0 / 3.0
LANES = 128
F32 = jnp.float32
BF16 = jnp.bfloat16
PAIRS = BLK // 2
VROWS = BLK * NV // LANES
TROWS = BLK * NC // LANES
VM = pl.BlockSpec(memory_space=pltpu.VMEM)
SM = pl.BlockSpec(memory_space=pltpu.SMEM)
HB = pl.BlockSpec(memory_space=pltpu.HBM)
LIMIT = 16 * 1024 * 1024


def lane_iota(rows):
    return lax.broadcasted_iota(jnp.int32, (rows, LANES), 1)


def row_iota(rows):
    return lax.broadcasted_iota(jnp.int32, (rows, LANES), 0)


def roll(x, shift):
    return pltpu.roll(x, shift, 1)


def upper(x):
    return x.astype(BF16).astype(F32)


def hi_lo_lanes(x):
    return x - jnp.where(lane_iota(x.shape[0]) < 64, 0.0, upper(x))


def split(x):
    hi = x.astype(BF16)
    return jnp.concatenate([hi, (x - hi.astype(F32)).astype(BF16)], axis=0)


def rows_to_columns(rows, fold_ref, spread_ref):
    group = lane_iota(VROWS) // NV
    for s in range(4):
        spread_ref[pl.ds(s, VROWS, stride=4), :] = jnp.where(group == s, rows, 0.0)
    x = mm_t(fold_ref[...], split(spread_ref[...]))
    return x + roll(x, 64)


def pack_columns(x):
    return jnp.where(lane_iota(VROWS) < 64, x[:VROWS], x[VROWS:])


def unpack_columns(x):
    low = lane_iota(VROWS) < 64
    turned = roll(x, 64)
    return jnp.concatenate([jnp.where(low, x, turned), jnp.where(low, turned, x)], axis=0)


def mm_t(a, b):
    return lax.dot_general(a, b, (((1,), (1,)), ((), ())), preferred_element_type=F32)


def mm(a, b):
    return jnp.dot(a, b, preferred_element_type=F32)


def pick_rows(parts):
    sub, lane = row_iota(8), lane_iota(8)
    step = 4
    while len(parts) > 1:
        half = len(parts) // 2
        first = (sub & step) == 0
        same = first == ((lane & step) == 0)
        merged = []
        for u in range(half):
            a, b = parts[u], parts[u + half]
            other = jnp.where(first, b, a)
            turned = pltpu.roll(other, step, 0)
            if step < 4:
                turned = jnp.where(first, pltpu.roll(other, 8 - step, 0), turned)
            merged.append(jnp.where(same, jnp.where(first, a, b), turned))
        parts = merged
        step //= 2
    return parts[0]


def neighbour(near_ref, b, i, j, k, wide):
    return (i + 1) * wide + j + 1 if k == 0 else near_ref[b * (KS + 1) + k]


def edge_kernel(height, across, meta_ref, tv_ref, ea_ref, eb_ref, ra_ref, rb_ref):
    row_a, row_b, col_a, col_b = halo_slots(meta_ref, height, across)
    for ref, col in ((ea_ref, col_a), (eb_ref, col_b)):
        j = jnp.where(col == 0, 0, across - 1)
        ref[...] = tv_ref[pl.ds(j, height * VROWS, stride=across), :]
    for ref, row in ((ra_ref, row_a), (rb_ref, row_b)):
        start = jnp.where(row == 0, 0, height - 1) * VROWS * across
        for j in range(across):
            ref[j * VROWS : (j + 1) * VROWS, :] = tv_ref[pl.ds(start + j, VROWS, stride=across), :]


def prepare_kernel(across, start, stop, ints_ref, a_hbm, tv_ref, fold_ref, turn_ref, *refs):
    at_ref, rd_ref, v_ref, buf, rep_ref, sem = refs[-6:]
    tiles = KS * PAIRS
    chunk = tiles * across
    depth = buf.shape[0]

    def copy(i):
        slot = lax.rem(i, depth)
        return pltpu.make_async_copy(
            a_hbm.at[pl.ds(i * chunk, chunk), :], buf.at[slot], sem.at[slot]
        )

    for i in range(depth - 1):
        copy(start + i).start()
    low = lane_iota(2 * PAIRS) < 64
    lane = lane_iota(PAIRS)
    on_diagonal = (lane & (BLK - 1)) == 2 * row_iota(PAIRS) + lane // BLK

    def body(i, carry):
        @pl.when(i + depth - 1 < stop)
        def _():
            copy(i + depth - 1).start()

        copy(i).wait()
        slot = lax.rem(i, depth)
        for j in range(across):
            b = i * across + j

            def part(k):
                return buf[slot, pl.ds(k * PAIRS * across + j, PAIRS, stride=across), :]

            for first, slots in ((0, 2), (2, 2), (4, 1)):
                halves = []
                for k in range(first, first + slots):
                    x = part(k)
                    if k == 0:
                        d = jnp.sum(jnp.where(on_diagonal, x, 0.0), axis=0, keepdims=True)
                        rd_ref[pl.ds(b, 1), :] = OMEGA / (d + roll(d, 64))
                    m = split(x)
                    zero = jnp.zeros_like(m)
                    halves += [jnp.where(low, m, zero), jnp.where(low, zero, m)]
                y = mm_t(turn_ref[...], jnp.concatenate(halves, axis=0)).astype(BF16)
                for u in range(slots):
                    k = first + u
                    at_ref[b, k * BLK : (k + 1) * BLK, :] = y[:, u * LANES : (u + 1) * LANES]
            v_ref[pl.ds(b * NV, NV), :] = rows_to_columns(
                tv_ref[pl.ds(i * VROWS * across + j, VROWS, stride=across), :],
                fold_ref, rep_ref.at[j],
            )
        return carry

    lax.fori_loop(start, stop, body, 0)


def halo_slots(meta_ref, height, across):
    slab_odd, pencil_odd = meta_ref[0], meta_ref[1]
    col_a = jnp.where(pencil_odd == 0, across + 1, 0)
    row_a = jnp.where(slab_odd == 0, height + 1, 0)
    return row_a, height + 1 - row_a, col_a, across + 1 - col_a


def fill_own(height, across, v_ref, u_ref):
    wide = across + 2

    def own(i, carry):
        for j in range(across):
            u_ref[(i + 1) * wide + j + 1] = split(v_ref[pl.ds((i * across + j) * NV, NV), :])
        return carry

    lax.fori_loop(0, height, own, 0, unroll=2)


def fill_pencil(height, across, meta_ref, pencil, u_ref, convert):
    wide = across + 2
    _, _, col_a, col_b = halo_slots(meta_ref, height, across)

    def side(i, carry):
        for s, (ref, col) in enumerate(zip(pencil, (col_a, col_b))):
            u_ref[(i + 1) * wide + col] = split(convert(ref[pl.ds(i * VROWS, VROWS), :], s))
        return carry

    lax.fori_loop(0, height, side, 0, unroll=4)


def fill_slab(height, across, meta_ref, slab, u_ref, convert):
    wide = across + 2
    row_a, row_b, col_a, col_b = halo_slots(meta_ref, height, across)
    for s, (ref, row) in enumerate(zip(slab, (row_a, row_b))):
        for j in range(wide):
            col = j + 1 if j < across else (col_a if j == across else col_b)
            u_ref[row * wide + col] = split(
                convert(ref[j * VROWS : (j + 1) * VROWS, :], (s * wide + j) % across)
            )


def sweep_rows(height, across, first, last, columns, near_ref, at_ref, rd_ref, v_ref, u_ref, out_ref):
    wide = across + 2
    low = lane_iota(2 * NV) < 64
    cell = lane_iota(NV) & (BLK - 1)
    stored = (cell & 1) * BLK + cell // 2

    def body(i, carry):
        for j in columns:
            b = i * across + j
            u = [u_ref[neighbour(near_ref, b, i, j, k, wide)] for k in range(KS)]
            left = jnp.concatenate(
                [jnp.where(low, u[0], u[1]), jnp.where(low, u[2], u[3]), u[4][:, :BLK]], axis=1
            )
            r = mm(left, at_ref[b])
            s = r[:NV] + r[NV:]
            s = jnp.take_along_axis(s, stored, axis=1) + jnp.take_along_axis(s, stored + PAIRS, axis=1)
            at = pl.ds(b * NV, NV)
            out_ref[at, :] = v_ref[at, :] - s * rd_ref[pl.ds(b, 1), :]
        return carry

    if last is None:
        for i in first:
            body(i, 0)
    else:
        lax.fori_loop(first, last, body, 0, unroll=7 if (last - first) % 7 == 0 else 4)


def sweep_kernel(height, across, near_ref, meta_ref, at_ref, rd_ref, v_ref, pa, pb, sa, sb, fold_ref,
                 out_ref, ea_ref, eb_ref, ra_ref, rb_ref, u_ref, rep_ref):
    def convert(rows, slot):
        return rows_to_columns(rows, fold_ref, rep_ref.at[slot])

    fill_own(height, across, v_ref, u_ref)
    fill_pencil(height, across, meta_ref, (pa, pb), u_ref, lambda rows, s: convert(rows, s))
    fill_slab(height, across, meta_ref, (sa, sb), u_ref, convert)
    sweep_rows(height, across, 0, height, range(across), near_ref, at_ref, rd_ref, v_ref, u_ref, out_ref)
    row_a, row_b, col_a, col_b = halo_slots(meta_ref, height, across)

    def message(i, j):
        return pack_columns(out_ref[pl.ds((i * across + j) * NV, NV), :])

    def edge(i, carry):
        for ref, col in ((ea_ref, col_a), (eb_ref, col_b)):
            ref[pl.ds(i * VROWS, VROWS), :] = message(i, jnp.where(col == 0, 0, across - 1))
        return carry

    lax.fori_loop(0, height, edge, 0)
    for ref, row in ((ra_ref, row_a), (rb_ref, row_b)):
        i = jnp.where(row == 0, 0, height - 1)
        for j in range(across):
            ref[j * VROWS : (j + 1) * VROWS, :] = message(i, j)


def unpack_received(rows, slot):
    return unpack_columns(rows)


def coefficients(across, capacity, per_owner, i, acc, agg_ref, modes_ref, out_ref, pay_ref):
    hcount = -(-capacity // 4)
    slot_rows = hcount * NC + 1
    values = [out_ref[pl.ds((i * across + j) * NV, NV), :] for j in range(across)]
    for v in values:
        acc = acc + v * v
    for g in range(across // capacity):
        owner = lax.div(agg_ref[(i * across + g * capacity) * (KS + 1) + KS], per_owner)
        for h in range(hcount):
            upper_rows, lower_rows = [], []
            for s in range(4):
                if h * 4 + s < capacity:
                    both = split(values[g * capacity + h * 4 + s])
                else:
                    both = jnp.zeros((2 * NV, LANES), BF16)
                upper_rows.append(both[:NV])
                lower_rows.append(both[NV:])
            r = mm_t(modes_ref[...], jnp.concatenate(upper_rows + lower_rows, axis=0))
            pay_ref[pl.ds(owner * slot_rows + h * NC, NC), :] = r[:NC, :LANES] + r[:NC, LANES:]
    return acc


def inner_sweep_kernel(height, across, near_ref, meta_ref, at_ref, rd_ref, v_ref, out_ref, u_ref, mark_ref):
    fill_own(height, across, v_ref, u_ref)
    sweep_rows(height, across, 1, height - 1, range(1, across - 1), near_ref, at_ref, rd_ref, v_ref,
               u_ref, out_ref)
    mark_ref[...] = jnp.zeros(mark_ref.shape, F32)


def side_sweep_kernel(height, across, capacity, per_owner, near_ref, meta_ref, at_ref, rd_ref, v_ref,
                      pa, pb, modes_ref, out_in, u_in, out_ref, u_ref, pay_ref, acc_ref):
    fill_pencil(height, across, meta_ref, (pa, pb), u_ref, unpack_received)
    sweep_rows(height, across, 1, height - 1, (0, across - 1), near_ref, at_ref, rd_ref, v_ref,
               u_ref, out_ref)
    pay_ref[...] = jnp.zeros(pay_ref.shape, F32)

    def coefs(i, acc):
        return coefficients(across, capacity, per_owner, i, acc, near_ref, modes_ref, out_ref, pay_ref)

    acc_ref[...] = lax.fori_loop(1, height - 1, coefs, jnp.zeros((NV, LANES), F32), unroll=2)


def outer_sweep_kernel(height, across, capacity, per_owner, near_ref, meta_ref, at_ref, rd_ref, v_ref,
                       sa, sb, modes_ref, acc_ref, out_in, u_in, pay_in, out_ref, u_ref, pay_ref):
    hcount = -(-capacity // 4)
    slot_rows = hcount * NC + 1
    devices = pay_ref.shape[0] // slot_rows
    fill_slab(height, across, meta_ref, (sa, sb), u_ref, unpack_received)
    sweep_rows(height, across, (0, height - 1), None, range(across), near_ref, at_ref, rd_ref, v_ref, u_ref, out_ref)
    acc = acc_ref[...]
    for i in (0, height - 1):
        acc = coefficients(across, capacity, per_owner, i, acc, near_ref, modes_ref, out_ref, pay_ref)
    square = jnp.concatenate([acc, jnp.zeros((LANES - NV, LANES), F32)], axis=0)
    total = 0.5 * jnp.sum(jnp.transpose(square), axis=0, keepdims=True)
    pay_ref[pl.ds(slot_rows - 1, devices, stride=slot_rows), :] = jnp.where(
        lane_iota(devices) < NV, total, -1.0
    )
    lane = lane_iota(1)

    def mark(g, carry):
        owner = lax.div(near_ref[g * capacity * (KS + 1) + KS], per_owner)
        row = jnp.where(lane < NV, total, -1.0)
        for s in range(capacity):
            local = near_ref[(g * capacity + s) * (KS + 1) + KS] - owner * per_owner
            row = jnp.where(lane == NV + s, local.astype(F32), row)
        pay_ref[pl.ds(owner * slot_rows + slot_rows - 1, 1), :] = row
        return carry

    lax.fori_loop(0, height * across // capacity, mark, 0, unroll=4)


def solve_kernel(cells, per_owner, capacity, got_ref, ret_ref, inv_ref):
    hcount = -(-capacity // 4)
    slot_rows = hcount * NC + 1
    devices = got_ref.shape[0] // slot_rows
    lane = lane_iota(devices)
    extra = got_ref[pl.ds(slot_rows - 1, devices, stride=slot_rows), :]
    total = jnp.sum(jnp.where(lane < NV, extra, 0.0), axis=0, keepdims=True)
    total = jnp.broadcast_to(total, (8, LANES))
    total = total + roll(total, NV)
    total = total + roll(total, 64)
    inv = 1.0 / jnp.sqrt(total / cells + 1e-06)
    inv_ref[...] = jnp.transpose(jnp.broadcast_to(inv[0:1], (LANES, LANES)))[:NV]
    width = 4 * per_owner
    inner = lane & (width - 1)
    hot = []
    for h in range(hcount):
        want = jnp.full((devices, LANES), -1.0, F32)
        for s in range(min(4, capacity - 4 * h)):
            column = extra[:, NV + 4 * h + s : NV + 4 * h + s + 1]
            want = jnp.where(inner // per_owner == s, column, want)
        same = want == (inner & (per_owner - 1)).astype(F32)
        hot.append(jnp.where(same & (lane < 2 * width), 1.0, 0.0))
    hot = jnp.concatenate(hot, axis=0)
    hot_t = jnp.transpose(hot)[:width]
    parts = [
        jnp.concatenate(
            [got_ref[pl.ds(h * NC + m, devices, stride=slot_rows), :] for h in range(hcount)], axis=0
        )
        for m in range(NC)
    ]
    data = jnp.concatenate(parts, axis=1)
    ones = jnp.ones((hcount * devices, LANES), F32)
    high = jnp.concatenate([data, ones], axis=1).astype(BF16)
    rest = jnp.concatenate([data - upper(data), jnp.zeros_like(ones)], axis=1).astype(BF16)
    hot_b = hot_t.astype(BF16)
    sums = mm(hot_b, high) + mm(hot_b, rest)
    group_lane = lane_iota(per_owner) // NV

    def block(s, m):
        return sums[s * per_owner : (s + 1) * per_owner, m * LANES : (m + 1) * LANES]

    count = sum(block(s, NC) for s in range(4))
    weight = inv[0:1] / jnp.maximum(count, 1.0)
    coarse = []
    for m in range(NC):
        c = jnp.zeros((per_owner, LANES), F32)
        for s in range(4):
            c = jnp.where(group_lane == s, block(s, m), c)
        c = c + roll(c, NV)
        c = c + roll(c, 64)
        coarse.append(c * weight)

    def dot_all(x):
        for shift in (16, 8, 4, 2, 1):
            x = x + roll(x, shift)
        return x

    gram = {(a, c): dot_all(coarse[a] * coarse[c]) for a in range(NC) for c in range(a + 1)}
    ridge = 0.1 * sum(gram[m, m] for m in range(NC)) / NC + 1e-06
    for m in range(NC):
        gram[m, m] = gram[m, m] + ridge
    recip = []
    for m in range(NC):
        root = 1.0 / jnp.sqrt(gram[m, m])
        recip.append(root)
        for a in range(m + 1, NC):
            gram[a, m] = gram[a, m] * root
        for a in range(m + 1, NC):
            for c in range(m + 1, a + 1):
                gram[a, c] = gram[a, c] - gram[a, m] * gram[c, m]
    solved = list(coarse)
    for m in range(NC):
        solved[m] = solved[m] * recip[m]
        for a in range(m + 1, NC):
            solved[a] = solved[a] - gram[a, m] * solved[m]
    for m in reversed(range(NC)):
        solved[m] = solved[m] * recip[m]
        for a in range(m):
            solved[a] = solved[a] - gram[m, a] * solved[m]
    table = jnp.concatenate(
        [
            jnp.concatenate([jnp.where(group_lane == s, solved[m], 0.0) for s in range(4)], axis=0)
            for m in range(NC)
        ],
        axis=1,
    )
    stacked = jnp.concatenate([table.astype(BF16), (table - upper(table)).astype(BF16)], axis=0)
    back = mm(hot[:, : 2 * width].astype(BF16), stacked)
    for h in range(hcount):
        for m in range(NC):
            ret_ref[pl.ds(h * NC + m, devices, stride=hcount * NC), :] = back[
                h * devices : (h + 1) * devices, m * LANES : (m + 1) * LANES
            ]


def relaxed_kernel(height, across, v_ref, inv_ref, order_ref, after_ref, rel_ref):
    inv = inv_ref[...]
    group = lane_iota(VROWS) // NV

    def body(i, carry):
        for j in range(across):
            both = split(v_ref[pl.ds((i * across + j) * NV, NV), :] * inv)
            r = mm_t(order_ref[...], jnp.concatenate([both, both], axis=0))
            r = r + roll(r, NV)
            rows = r[:VROWS]
            for s in range(1, 4):
                rows = jnp.where(group == s, r[s * VROWS : (s + 1) * VROWS], rows)
            rel_ref[pl.ds(i * VROWS * across + j, VROWS, stride=across), :] = rows
        return carry

    lax.fori_loop(0, height, body, 0, unroll=4)


def cell_rows(parts, place_ref):
    x = jnp.concatenate([x for part in parts for x in part], axis=0)
    hi = x.astype(BF16)
    r = mm(jnp.concatenate([hi, (x - hi.astype(F32)).astype(BF16)], axis=1), place_ref[...])
    out = []
    for n in range(len(parts)):
        for q in range(TROWS):
            out.append(
                pick_rows(
                    [
                        r[(n * 8 + u) * 8 : (n * 8 + u + 1) * 8, q * LANES : (q + 1) * LANES]
                        for u in range(8)
                    ]
                )
            )
    return out


def tile_kernel(height, across, capacity, per_owner, meta_ref, agg_ref, ret_ref, v_ref, inv_ref, place_ref,
                tile_ref, out_ref, ea_ref, eb_ref, ra_ref, rb_ref):
    hcount = -(-capacity // 4)
    group_lane = lane_iota(NC) // NV
    inv = inv_ref[...]

    def body(i, carry):
        tiles = []
        for g in range(across // capacity):
            owner = lax.div(agg_ref[(i * across + g * capacity) * (KS + 1) + KS], per_owner)
            for h in range(hcount):
                m = ret_ref[pl.ds(pl.multiple_of((owner * hcount + h) * NC, NC), NC), :]
                m_hi = upper(m)
                left = jnp.concatenate(
                    [jnp.where(group_lane == s, x, 0.0) for x in (m_hi, m - m_hi) for s in range(4)],
                    axis=0,
                ).astype(BF16)
                upper_rows, lower_rows = [], []
                for s in range(4):
                    if h * 4 + s < capacity:
                        b = i * across + g * capacity + h * 4 + s
                        both = split(v_ref[pl.ds(b * NV, NV), :] * inv)
                    else:
                        both = jnp.zeros((2 * NV, LANES), BF16)
                    upper_rows.append(both[:NV])
                    lower_rows.append(both[NV:])
                r = mm(
                    jnp.concatenate([left, left], axis=1),
                    jnp.concatenate(upper_rows + lower_rows, axis=0),
                )
                for s in range(min(4, capacity - h * 4)):
                    t = r[s * NC : (s + 1) * NC] + r[(4 + s) * NC : (5 + s) * NC]
                    b = i * across + g * capacity + h * 4 + s
                    tile_ref[pl.ds(b * NC, NC), :] = t
                    tiles.append(t)
        return carry

    lax.fori_loop(0, height, body, 0, unroll=2)
    step = 4 if height % 4 == 0 else 1

    def rows(s, carry):
        parts = [
            [tile_ref[pl.ds(((s * step + i) * across + j) * NC, NC), :] for j in range(across)]
            for i in range(step)
        ]
        for n, x in enumerate(cell_rows(parts, place_ref)):
            at = pl.multiple_of((s * step * TROWS + n) * across, 8)
            out_ref[pl.ds(at, across), :] = x
        return carry

    lax.fori_loop(0, height // step, rows, 0)
    row_a, row_b, col_a, col_b = halo_slots(meta_ref, height, across)

    def edge(i, carry):
        for ref, col in ((ea_ref, col_a), (eb_ref, col_b)):
            j = jnp.where(col == 0, 0, across - 1)
            ref[pl.ds(i * NC, NC), :] = tile_ref[pl.ds((i * across + j) * NC, NC), :]
        return carry

    lax.fori_loop(0, height, edge, 0)
    for ref, row in ((ra_ref, row_a), (rb_ref, row_b)):
        i = jnp.where(row == 0, 0, height - 1)
        ref[...] = tile_ref[pl.ds(pl.multiple_of(i * across * NC, 8), across * NC), :]


def product_kernel(height, across, near_ref, meta_ref, at_ref, tile_ref, pa_ref, pb_ref, sa_ref, sb_ref,
                   place_ref, out_ref, u_ref):
    wide = across + 2
    row_a, row_b, col_a, col_b = halo_slots(meta_ref, height, across)
    low = lane_iota(NC) < 64

    def put(index, x):
        hi = upper(x)
        lo = x - hi
        u_ref[index] = jnp.concatenate(
            [
                jnp.where(low, hi, 0.0), jnp.where(low, lo, 0.0),
                jnp.where(low, 0.0, hi), jnp.where(low, 0.0, lo),
            ],
            axis=0,
        ).astype(BF16)

    def own(i, carry):
        for j in range(across):
            put((i + 1) * wide + j + 1, tile_ref[pl.ds((i * across + j) * NC, NC), :])
        for ref, col in ((pa_ref, col_a), (pb_ref, col_b)):
            put((i + 1) * wide + col, ref[pl.ds(i * NC, NC), :])
        return carry

    lax.fori_loop(0, height, own, 0)
    for ref, row in ((sa_ref, row_a), (sb_ref, row_b)):
        for j in range(wide):
            col = j + 1 if j < across else (col_a if j == across else col_b)
            put(row * wide + col, ref[j * NC : (j + 1) * NC, :])

    def body(i, carry):
        parts = [[] for _ in range(KS)]
        for j in range(across):
            b = i * across + j
            u = [
                u_ref[neighbour(near_ref, b, i, j, k, wide), (k % 2) * 2 * NC : (k % 2 + 1) * 2 * NC, :]
                for k in range(KS)
            ]
            for t in range(3):
                left = jnp.concatenate(u[2 * t : 2 * t + 2], axis=0)
                if t < 2:
                    r = mm(left, at_ref[b, t * LANES : (t + 1) * LANES, :])
                else:
                    r = mm(left[:, :BLK], at_ref[b, 2 * LANES : 2 * LANES + BLK, :])
                for s in range(left.shape[0] // (2 * NC)):
                    parts[2 * t + s].append(
                        r[s * 2 * NC : s * 2 * NC + NC] + r[s * 2 * NC + NC : (s + 1) * 2 * NC]
                    )
        for n, rows in enumerate(cell_rows(parts, place_ref)):
            at = pl.multiple_of((i * KS * TROWS + n) * across, 8)
            out_ref[pl.ds(at, across), :] = rows
        return carry

    lax.fori_loop(0, height, body, 0, unroll=4)


def swaps(count, first):
    pairs = [(i, i + 1) for i in range(first, count - 1, 2)]
    return pairs + [(b, a) for a, b in pairs]


def exchange(edges, rows, slab_odd, unit, height, work=None):
    pencils, slabs = lax.axis_size("pencil"), lax.axis_size("slab")
    got = [lax.ppermute(e, "pencil", swaps(pencils, s)) for s, e in enumerate(edges)]
    done = work() if work else None
    messages = []
    for s, own in enumerate(rows):
        last = (slab_odd == 0) if s == 0 else (slab_odd == 1)
        corners = [
            jnp.where(last, g[(height - 1) * unit : height * unit], g[:unit]) for g in got
        ]
        messages.append(jnp.concatenate([own] + corners, axis=0))
    if work:
        messages = [m + done[-1] for m in messages]
    out = [lax.ppermute(m, "slab", swaps(slabs, s)) for s, m in enumerate(messages)]
    return got + out, messages, done


def lines(x, features):
    height, across, _ = x.shape
    y = x.reshape(height, across, features // LANES, LANES).transpose(0, 2, 1, 3)
    return y.reshape(height * across * features // LANES, LANES)


def unlines(y, height, across, features):
    x = y.reshape(height, features // LANES, across, LANES).transpose(0, 2, 1, 3)
    return x.reshape(height, across, features)


def call(kernel, outs, ins, scratch=(), limit=LIMIT, specs=None, aliases=None):
    return pl.pallas_call(
        kernel,
        out_shape=outs,
        in_specs=specs,
        out_specs=[VM] * len(outs),
        scratch_shapes=list(scratch),
        input_output_aliases=aliases or {},
        compiler_params=pltpu.CompilerParams(vmem_limit_bytes=limit),
    )(*ins)


def sds(*shape, dtype=F32):
    return jax.ShapeDtypeStruct(shape, dtype)


def mode_table():
    centre = np.arange(BLK, dtype=np.float64) + 0.5
    q = np.cos(math.pi * centre[:, None] * np.arange(NC)[None, :] / BLK).astype(np.float32)
    return q


def shards(a_blocks, col_codes, agg_of, test_vectors):
    height, across = agg_of.shape
    slabs, pencils = lax.axis_size("slab"), lax.axis_size("pencil")
    devices = slabs * pencils
    block_rows = height * across
    capacity = 2 * block_rows // devices
    per_owner = block_rows // 8
    hcount = -(-capacity // 4)
    wide = across + 2
    slab_odd = lax.axis_index("slab") % 2
    pencil_odd = lax.axis_index("pencil") % 2
    meta = jnp.stack([slab_odd, pencil_odd]).astype(jnp.int32)
    down = jnp.arange(height, dtype=jnp.int32)[:, None, None] + col_codes // 3
    near = down * wide + jnp.arange(across, dtype=jnp.int32)[None, :, None] + col_codes % 3
    ints = jnp.concatenate([near, agg_of[:, :, None]], axis=2).reshape(-1)

    tv = lines(test_vectors, BLK * NV)
    *edges, row_one, row_two = call(
        functools.partial(edge_kernel, height, across),
        [sds(height * VROWS, LANES)] * 2 + [sds(across * VROWS, LANES)] * 2,
        [meta, tv],
        specs=[SM, VM],
    )
    rows = [row_one, row_two]

    lane = np.arange(LANES)
    fold = jnp.asarray(np.arange(NV)[:, None] == lane[None, :] % NV, BF16)
    place_to = np.arange(TROWS * LANES) // NC
    place_one = ((lane[:, None] % BLK) == place_to[None, :]) & (lane[:, None] < BLK)
    place = jnp.asarray(np.concatenate([place_one, place_one], axis=0), BF16)
    turn = jnp.asarray(np.arange(BLK)[:, None] == lane[None, :] % BLK, BF16)
    stored = 2 * (lane % PAIRS) + lane // BLK
    place_one = stored[:, None] == place_to[None, :]
    place_stored = jnp.asarray(np.concatenate([place_one, place_one], axis=0), BF16)
    order_row = np.arange(BLK)
    order = jnp.asarray(((order_row % VROWS) * 4 + order_row // VROWS)[:, None] == lane[None, :], BF16)
    q = mode_table()
    q_hi = jnp.asarray(q.T).astype(BF16)
    q_lo = (jnp.asarray(q.T) - q_hi.astype(F32)).astype(BF16)
    modes = jnp.pad(jnp.concatenate([q_hi, q_lo], axis=1), ((0, NC), (0, 0)))

    chunk = KS * PAIRS * across
    stored_blocks = pltpu.with_memory_space_constraint(lines(a_blocks, KS * BLK * BLK), pltpu.HBM)

    def prepare(start, stop, earlier, after=()):
        count = 5 + len(after)
        return call(
            functools.partial(prepare_kernel, across, start, stop),
            [
                sds(block_rows, KS * BLK, LANES, dtype=BF16),
                sds(block_rows, LANES),
                sds(block_rows * NV, LANES),
            ],
            [ints, stored_blocks, tv, fold, turn, *after, *earlier],
            [
                pltpu.VMEM((4, chunk, LANES), F32),
                pltpu.VMEM((across, BLK, LANES), F32),
                pltpu.SemaphoreType.DMA((4,)),
            ],
            specs=[SM, HB, VM, VM, VM] + [HB] * len(after) + [VM] * len(earlier),
            aliases={count + n: n for n in range(len(earlier))},
        )

    halo, sent, _ = exchange(edges, rows, slab_odd, VROWS, height)
    at, rd, v = prepare(0, height, [], sent)
    field = [pltpu.VMEM((wide * (height + 2), 2 * NV, LANES), BF16)]
    v, ea, eb, ra, rb = call(
        functools.partial(sweep_kernel, height, across),
        [sds(block_rows * NV, LANES)] + [sds(height * VROWS, LANES)] * 2 + [sds(across * VROWS, LANES)] * 2,
        [ints, meta, at, rd, v, *halo, fold],
        field + [pltpu.VMEM((across, BLK, LANES), F32)],
        specs=[SM, SM] + [VM] * 8,
    )
    outs = [
        sds(block_rows * NV, LANES),
        sds(wide * (height + 2), 2 * NV, LANES, dtype=BF16),
    ]
    halo, _, partial = exchange(
        [ea, eb], [ra, rb], slab_odd, VROWS, height,
        lambda: call(
            functools.partial(inner_sweep_kernel, height, across),
            outs + [sds(wide * VROWS, LANES)],
            [ints, meta, at, rd, v],
            specs=[SM, SM] + [VM] * 3,
        ),
    )
    slot_rows = hcount * NC + 1
    outs = outs + [sds(devices * slot_rows, LANES)]
    sizes = (height, across, capacity, per_owner)
    *partial, acc = call(
        functools.partial(side_sweep_kernel, *sizes),
        outs + [sds(NV, LANES)],
        [ints, meta, at, rd, v, *halo[:2], modes, *partial[:2]],
        specs=[SM, SM] + [VM] * 8,
        aliases={8: 0, 9: 1},
    )
    v, _, pay = call(
        functools.partial(outer_sweep_kernel, *sizes),
        outs,
        [ints, meta, at, rd, v, *halo[2:], modes, acc, *partial],
        specs=[SM, SM] + [VM] * 10,
        aliases={9: 0, 10: 1, 11: 2},
    )
    got = lax.all_to_all(
        pay.reshape(devices, slot_rows * LANES), ("slab", "pencil"), split_axis=0, concat_axis=0, tiled=True
    ).reshape(devices * slot_rows, LANES)
    ret, inv = call(
        functools.partial(solve_kernel, float(block_rows * BLK * devices), per_owner, capacity),
        [sds(devices * hcount * NC, LANES), sds(NV, LANES)],
        [got],
        specs=[VM],
    )
    back = lax.all_to_all(
        ret.reshape(devices, hcount * NC * LANES), ("slab", "pencil"), split_axis=0, concat_axis=0, tiled=True
    ).reshape(devices * hcount * NC, LANES)
    tile, tiles, ea, eb, ra, rb = call(
        functools.partial(tile_kernel, height, across, capacity, per_owner),
        [sds(block_rows * NC, LANES), sds(block_rows * TROWS, LANES)]
        + [sds(height * NC, LANES)] * 2 + [sds(across * NC, LANES)] * 2,
        [meta, ints, back, v, inv, place],
        specs=[SM, SM, VM, VM, VM, VM],
    )
    (relaxed,) = call(
        functools.partial(relaxed_kernel, height, across),
        [sds(block_rows * VROWS, LANES)],
        [v, inv, order, tile],
        specs=[VM] * 4,
    )
    halo, _, _ = exchange([ea, eb], [ra, rb], slab_odd, NC, height)
    (products,) = call(
        functools.partial(product_kernel, height, across),
        [sds(block_rows * KS * TROWS, LANES)],
        [ints, meta, at, tile, *halo, place_stored],
        [pltpu.VMEM((wide * (height + 2), 4 * NC, LANES), BF16)],
        specs=[SM, SM] + [VM] * 7,
    )
    return (
        unlines(relaxed, height, across, BLK * NV),
        unlines(tiles, height, across, BLK * NC),
        unlines(products, height, across, KS * BLK * NC),
    )


def solution(mesh):
    in_specs = (P("slab", "pencil", None), P("slab", "pencil", None), P("slab", "pencil"), P("slab", "pencil", None))
    out_specs = (P("slab", "pencil", None),) * 3
    return jax.shard_map(shards, mesh=mesh, in_specs=in_specs, out_specs=out_specs, check_vma=False)
```

```python
import functools
import math

import jax
import jax.numpy as jnp
import numpy as np
from jax import lax
from jax.experimental import pallas as pl
from jax.experimental.pallas import tpu as pltpu
from jax.sharding import PartitionSpec as P


BLK = 64
NV = 32
NC = 8
KS = 5
OMEGA = 2.0 / 3.0
LANES = 128
F32 = jnp.float32
BF16 = jnp.bfloat16
PAIRS = BLK // 2
VROWS = BLK * NV // LANES
TROWS = BLK * NC // LANES
VM = pl.BlockSpec(memory_space=pltpu.VMEM)
SM = pl.BlockSpec(memory_space=pltpu.SMEM)
HB = pl.BlockSpec(memory_space=pltpu.HBM)
LIMIT = 16 * 1024 * 1024


def lane_iota(rows):
    return lax.broadcasted_iota(jnp.int32, (rows, LANES), 1)


def row_iota(rows):
    return lax.broadcasted_iota(jnp.int32, (rows, LANES), 0)


def roll(x, shift):
    return pltpu.roll(x, shift, 1)


def upper(x):
    return x.astype(BF16).astype(F32)


def split(x):
    hi = x.astype(BF16)
    return jnp.concatenate([hi, (x - hi.astype(F32)).astype(BF16)], axis=0)


def ones_at(rows, period):
    lane = lane_iota(rows) & (period - 1)
    return jnp.where(lane == row_iota(rows), 1.0, 0.0).astype(BF16)


def rows_to_columns(rows, fold, spread_ref):
    group = lane_iota(VROWS) // NV
    for s in range(4):
        spread_ref[pl.ds(s, VROWS, stride=4), :] = jnp.where(group == s, rows, 0.0)
    x = mm_t(fold, split(spread_ref[...]))
    return x + roll(x, 64)


def pack_columns(x):
    return jnp.where(lane_iota(VROWS) < 64, x[:VROWS], x[VROWS:])


def unpack_columns(x):
    low = lane_iota(VROWS) < 64
    turned = roll(x, 64)
    return jnp.concatenate([jnp.where(low, x, turned), jnp.where(low, turned, x)], axis=0)


def mm_t(a, b):
    return lax.dot_general(a, b, (((1,), (1,)), ((), ())), preferred_element_type=F32)


def mm(a, b):
    return jnp.dot(a, b, preferred_element_type=F32)


def pick_rows(parts):
    sub, lane = row_iota(8), lane_iota(8)
    step = 4
    while len(parts) > 1:
        half = len(parts) // 2
        first = (sub & step) == 0
        same = first == ((lane & step) == 0)
        merged = []
        for u in range(half):
            a, b = parts[u], parts[u + half]
            other = jnp.where(first, b, a)
            turned = pltpu.roll(other, step, 0)
            if step < 4:
                turned = jnp.where(first, pltpu.roll(other, 8 - step, 0), turned)
            merged.append(jnp.where(same, jnp.where(first, a, b), turned))
        parts = merged
        step //= 2
    return parts[0]


def neighbour(near_ref, b, i, j, k, wide):
    return (i + 1) * wide + j + 1 if k == 0 else near_ref[b * (KS + 1) + k]


def edge_kernel(height, across, meta_ref, tv_ref, ea_ref, eb_ref, ra_ref, rb_ref):
    row_a, row_b, col_a, col_b = halo_slots(meta_ref, height, across)
    for ref, col in ((ea_ref, col_a), (eb_ref, col_b)):
        j = jnp.where(col == 0, 0, across - 1)
        ref[...] = tv_ref[pl.ds(j, height * VROWS, stride=across), :]
    for ref, row in ((ra_ref, row_a), (rb_ref, row_b)):
        start = jnp.where(row == 0, 0, height - 1) * VROWS * across
        for j in range(across):
            ref[j * VROWS : (j + 1) * VROWS, :] = tv_ref[pl.ds(start + j, VROWS, stride=across), :]


def prepare_kernel(across, start, stop, ints_ref, a_hbm, tv_ref, *refs):
    fold, turn = ones_at(NV, NV), ones_at(BLK, BLK)
    at_ref, rd_ref, v_ref, buf, rep_ref, sem = refs[-6:]
    tiles = KS * PAIRS
    chunk = tiles * across
    depth = buf.shape[0]

    def copy(i):
        slot = lax.rem(i, depth)
        return pltpu.make_async_copy(
            a_hbm.at[pl.ds(i * chunk, chunk), :], buf.at[slot], sem.at[slot]
        )

    for i in range(depth - 1):
        copy(start + i).start()
    low = lane_iota(2 * PAIRS) < 64
    lane = lane_iota(PAIRS)
    on_diagonal = (lane & (BLK - 1)) == 2 * row_iota(PAIRS) + lane // BLK

    def body(i, carry):
        @pl.when(i + depth - 1 < stop)
        def _():
            copy(i + depth - 1).start()

        copy(i).wait()
        slot = lax.rem(i, depth)
        for j in range(across):
            b = i * across + j

            def part(k):
                return buf[slot, pl.ds(k * PAIRS * across + j, PAIRS, stride=across), :]

            for first, slots in ((0, 2), (2, 2), (4, 1)):
                halves = []
                for k in range(first, first + slots):
                    x = part(k)
                    if k == 0:
                        d = jnp.sum(jnp.where(on_diagonal, x, 0.0), axis=0, keepdims=True)
                        rd_ref[pl.ds(b, 1), :] = OMEGA / (d + roll(d, 64))
                    m = split(x)
                    zero = jnp.zeros_like(m)
                    halves += [jnp.where(low, m, zero), jnp.where(low, zero, m)]
                y = mm_t(turn, jnp.concatenate(halves, axis=0)).astype(BF16)
                for u in range(slots):
                    k = first + u
                    at_ref[b, k * BLK : (k + 1) * BLK, :] = y[:, u * LANES : (u + 1) * LANES]
            v_ref[pl.ds(b * NV, NV), :] = rows_to_columns(
                tv_ref[pl.ds(i * VROWS * across + j, VROWS, stride=across), :],
                fold, rep_ref.at[j],
            )
        return carry

    lax.fori_loop(start, stop, body, 0)


def halo_slots(meta_ref, height, across):
    slab_odd, pencil_odd = meta_ref[0], meta_ref[1]
    col_a = jnp.where(pencil_odd == 0, across + 1, 0)
    row_a = jnp.where(slab_odd == 0, height + 1, 0)
    return row_a, height + 1 - row_a, col_a, across + 1 - col_a


def fill_own(height, across, v_ref, u_ref):
    wide = across + 2

    def own(i, carry):
        for j in range(across):
            u_ref[(i + 1) * wide + j + 1] = split(v_ref[pl.ds((i * across + j) * NV, NV), :])
        return carry

    lax.fori_loop(0, height, own, 0, unroll=2)


def fill_pencil(height, across, meta_ref, pencil, u_ref, convert):
    wide = across + 2
    _, _, col_a, col_b = halo_slots(meta_ref, height, across)

    def side(i, carry):
        for s, (ref, col) in enumerate(zip(pencil, (col_a, col_b))):
            u_ref[(i + 1) * wide + col] = split(convert(ref[pl.ds(i * VROWS, VROWS), :], s))
        return carry

    lax.fori_loop(0, height, side, 0, unroll=4)


def fill_slab(height, across, meta_ref, slab, u_ref, convert):
    wide = across + 2
    row_a, row_b, col_a, col_b = halo_slots(meta_ref, height, across)
    for s, (ref, row) in enumerate(zip(slab, (row_a, row_b))):
        for j in range(wide):
            col = j + 1 if j < across else (col_a if j == across else col_b)
            u_ref[row * wide + col] = split(
                convert(ref[j * VROWS : (j + 1) * VROWS, :], (s * wide + j) % across)
            )


def sweep_rows(across, first, last, columns, near_ref, at_ref, rd_ref, v_ref, u_ref, out_ref):
    wide = across + 2
    low = lane_iota(2 * NV) < 64
    cell = lane_iota(NV) & (BLK - 1)
    stored = (cell & 1) * BLK + cell // 2

    def body(i, carry):
        for j in columns:
            b = i * across + j
            u = [u_ref[neighbour(near_ref, b, i, j, k, wide)] for k in range(KS)]
            left = jnp.concatenate(
                [jnp.where(low, u[0], u[1]), jnp.where(low, u[2], u[3]), u[4][:, :BLK]], axis=1
            )
            r = mm(left, at_ref[b])
            s = r[:NV] + r[NV:]
            s = jnp.take_along_axis(s, stored, axis=1) + jnp.take_along_axis(s, stored + PAIRS, axis=1)
            at = pl.ds(b * NV, NV)
            out_ref[at, :] = v_ref[at, :] - s * rd_ref[pl.ds(b, 1), :]
        return carry

    if last is None:
        for i in first:
            body(i, 0)
    else:
        lax.fori_loop(first, last, body, 0, unroll=7 if (last - first) % 7 == 0 else 8)


def sweep_kernel(height, across, near_ref, meta_ref, at_ref, rd_ref, v_ref, pa, pb, sa, sb,
                 out_ref, ea_ref, eb_ref, ra_ref, rb_ref, u_ref, rep_ref):
    fold = ones_at(NV, NV)

    def convert(rows, slot):
        return rows_to_columns(rows, fold, rep_ref.at[slot])

    fill_own(height, across, v_ref, u_ref)
    fill_pencil(height, across, meta_ref, (pa, pb), u_ref, lambda rows, s: convert(rows, s))
    fill_slab(height, across, meta_ref, (sa, sb), u_ref, convert)
    sweep_rows(across, 0, height, range(across), near_ref, at_ref, rd_ref, v_ref, u_ref, out_ref)
    row_a, row_b, col_a, col_b = halo_slots(meta_ref, height, across)

    def message(i, j):
        return pack_columns(out_ref[pl.ds((i * across + j) * NV, NV), :])

    def edge(i, carry):
        for ref, col in ((ea_ref, col_a), (eb_ref, col_b)):
            ref[pl.ds(i * VROWS, VROWS), :] = message(i, jnp.where(col == 0, 0, across - 1))
        return carry

    lax.fori_loop(0, height, edge, 0)
    for ref, row in ((ra_ref, row_a), (rb_ref, row_b)):
        i = jnp.where(row == 0, 0, height - 1)
        for j in range(across):
            ref[j * VROWS : (j + 1) * VROWS, :] = message(i, j)


def unpack_received(rows, slot):
    return unpack_columns(rows)


def coefficients(across, capacity, per_owner, i, acc, agg_ref, modes_ref, out_ref, pay_ref):
    hcount = -(-capacity // 4)
    slot_rows = hcount * NC + 1
    values = [out_ref[pl.ds((i * across + j) * NV, NV), :] for j in range(across)]
    for v in values:
        acc = acc + v * v
    for g in range(across // capacity):
        owner = lax.div(agg_ref[(i * across + g * capacity) * (KS + 1) + KS], per_owner)
        for h in range(hcount):
            upper_rows, lower_rows = [], []
            for s in range(4):
                if h * 4 + s < capacity:
                    both = split(values[g * capacity + h * 4 + s])
                else:
                    both = jnp.zeros((2 * NV, LANES), BF16)
                upper_rows.append(both[:NV])
                lower_rows.append(both[NV:])
            r = mm_t(modes_ref[...], jnp.concatenate(upper_rows + lower_rows, axis=0))
            pay_ref[pl.ds(owner * slot_rows + h * NC, NC), :] = r[:NC, :LANES] + r[:NC, LANES:]
    return acc


def inner_sweep_kernel(height, across, near_ref, meta_ref, at_ref, rd_ref, v_ref, out_ref, u_ref, mark_ref):
    fill_own(height, across, v_ref, u_ref)
    sweep_rows(across, 1, height - 1, range(1, across - 1), near_ref, at_ref, rd_ref, v_ref,
               u_ref, out_ref)
    mark_ref[...] = jnp.zeros(mark_ref.shape, F32)


def side_sweep_kernel(height, across, capacity, per_owner, near_ref, meta_ref, at_ref, rd_ref, v_ref,
                      pa, pb, modes_ref, out_in, u_in, out_ref, u_ref, pay_ref, acc_ref):
    fill_pencil(height, across, meta_ref, (pa, pb), u_ref, unpack_received)
    sweep_rows(across, 1, height - 1, (0, across - 1), near_ref, at_ref, rd_ref, v_ref,
               u_ref, out_ref)
    pay_ref[...] = jnp.zeros(pay_ref.shape, F32)

    def coefs(i, acc):
        return coefficients(across, capacity, per_owner, i, acc, near_ref, modes_ref, out_ref, pay_ref)

    acc_ref[...] = lax.fori_loop(1, height - 1, coefs, jnp.zeros((NV, LANES), F32), unroll=2)


def outer_sweep_kernel(height, across, capacity, per_owner, near_ref, meta_ref, at_ref, rd_ref, v_ref,
                       sa, sb, modes_ref, acc_ref, out_in, u_in, pay_in, out_ref, u_ref, pay_ref):
    hcount = -(-capacity // 4)
    slot_rows = hcount * NC + 1
    devices = pay_ref.shape[0] // slot_rows
    fill_slab(height, across, meta_ref, (sa, sb), u_ref, unpack_received)
    sweep_rows(across, (0, height - 1), None, range(across), near_ref, at_ref, rd_ref, v_ref, u_ref, out_ref)
    acc = acc_ref[...]
    for i in (0, height - 1):
        acc = coefficients(across, capacity, per_owner, i, acc, near_ref, modes_ref, out_ref, pay_ref)
    square = jnp.concatenate([acc, jnp.zeros((LANES - NV, LANES), F32)], axis=0)
    total = 0.5 * jnp.sum(jnp.transpose(square), axis=0, keepdims=True)
    pay_ref[pl.ds(slot_rows - 1, devices, stride=slot_rows), :] = jnp.where(
        lane_iota(devices) < NV, total, -1.0
    )
    lane = lane_iota(1)

    def mark(g, carry):
        owner = lax.div(near_ref[g * capacity * (KS + 1) + KS], per_owner)
        row = jnp.where(lane < NV, total, -1.0)
        for s in range(capacity):
            local = near_ref[(g * capacity + s) * (KS + 1) + KS] - owner * per_owner
            row = jnp.where(lane == NV + s, local.astype(F32), row)
        pay_ref[pl.ds(owner * slot_rows + slot_rows - 1, 1), :] = row
        return carry

    lax.fori_loop(0, height * across // capacity, mark, 0, unroll=4)


def solve_kernel(cells, per_owner, capacity, got_ref, ret_ref, inv_ref):
    hcount = -(-capacity // 4)
    slot_rows = hcount * NC + 1
    devices = got_ref.shape[0] // slot_rows
    lane = lane_iota(devices)
    extra = got_ref[pl.ds(slot_rows - 1, devices, stride=slot_rows), :]
    total = jnp.sum(jnp.where(lane < NV, extra, 0.0), axis=0, keepdims=True)
    total = jnp.broadcast_to(total, (8, LANES))
    total = total + roll(total, NV)
    total = total + roll(total, 64)
    inv = 1.0 / jnp.sqrt(total / cells + 1e-06)
    inv_ref[...] = jnp.transpose(jnp.broadcast_to(inv[0:1], (LANES, LANES)))[:NV]
    width = 4 * per_owner
    inner = lane & (width - 1)
    hot = []
    for h in range(hcount):
        want = jnp.full((devices, LANES), -1.0, F32)
        for s in range(min(4, capacity - 4 * h)):
            column = extra[:, NV + 4 * h + s : NV + 4 * h + s + 1]
            want = jnp.where(inner // per_owner == s, column, want)
        same = want == (inner & (per_owner - 1)).astype(F32)
        hot.append(jnp.where(same & (lane < 2 * width), 1.0, 0.0))
    hot = jnp.concatenate(hot, axis=0)
    hot_t = jnp.transpose(hot)[:width]
    parts = [
        jnp.concatenate(
            [got_ref[pl.ds(h * NC + m, devices, stride=slot_rows), :] for h in range(hcount)], axis=0
        )
        for m in range(NC)
    ]
    data = jnp.concatenate(parts, axis=1)
    ones = jnp.ones((hcount * devices, LANES), F32)
    high = jnp.concatenate([data, ones], axis=1).astype(BF16)
    rest = jnp.concatenate([data - upper(data), jnp.zeros_like(ones)], axis=1).astype(BF16)
    hot_b = hot_t.astype(BF16)
    sums = mm(hot_b, high) + mm(hot_b, rest)
    group_lane = lane_iota(per_owner) // NV

    def block(s, m):
        return sums[s * per_owner : (s + 1) * per_owner, m * LANES : (m + 1) * LANES]

    count = sum(block(s, NC) for s in range(4))
    weight = inv[0:1] / jnp.maximum(count, 1.0)
    coarse = []
    for m in range(NC):
        c = jnp.zeros((per_owner, LANES), F32)
        for s in range(4):
            c = jnp.where(group_lane == s, block(s, m), c)
        c = c + roll(c, NV)
        c = c + roll(c, 64)
        coarse.append(c * weight)

    def dot_all(x):
        for shift in (16, 8, 4, 2, 1):
            x = x + roll(x, shift)
        return x

    gram = {(a, c): dot_all(coarse[a] * coarse[c]) for a in range(NC) for c in range(a + 1)}
    ridge = 0.1 * sum(gram[m, m] for m in range(NC)) / NC + 1e-06
    for m in range(NC):
        gram[m, m] = gram[m, m] + ridge
    recip = []
    for m in range(NC):
        root = 1.0 / jnp.sqrt(gram[m, m])
        recip.append(root)
        for a in range(m + 1, NC):
            gram[a, m] = gram[a, m] * root
        for a in range(m + 1, NC):
            for c in range(m + 1, a + 1):
                gram[a, c] = gram[a, c] - gram[a, m] * gram[c, m]
    solved = list(coarse)
    for m in range(NC):
        solved[m] = solved[m] * recip[m]
        for a in range(m + 1, NC):
            solved[a] = solved[a] - gram[a, m] * solved[m]
    for m in reversed(range(NC)):
        solved[m] = solved[m] * recip[m]
        for a in range(m):
            solved[a] = solved[a] - gram[m, a] * solved[m]
    table = jnp.concatenate(
        [
            jnp.concatenate([jnp.where(group_lane == s, solved[m], 0.0) for s in range(4)], axis=0)
            for m in range(NC)
        ],
        axis=1,
    )
    stacked = jnp.concatenate([table.astype(BF16), (table - upper(table)).astype(BF16)], axis=0)
    back = mm(hot[:, : 2 * width].astype(BF16), stacked)
    for h in range(hcount):
        for m in range(NC):
            ret_ref[pl.ds(h * NC + m, devices, stride=hcount * NC), :] = back[
                h * devices : (h + 1) * devices, m * LANES : (m + 1) * LANES
            ]


def relaxed_kernel(height, across, v_ref, inv_ref, after_ref, rel_ref):
    row = row_iota(BLK)
    order = jnp.where(lane_iota(BLK) == (row % VROWS) * 4 + row // VROWS, 1.0, 0.0).astype(BF16)
    inv = inv_ref[...]
    group = lane_iota(VROWS) // NV

    def body(i, carry):
        for j in range(across):
            both = split(v_ref[pl.ds((i * across + j) * NV, NV), :] * inv)
            r = mm_t(order, jnp.concatenate([both, both], axis=0))
            r = r + roll(r, NV)
            rows = r[:VROWS]
            for s in range(1, 4):
                rows = jnp.where(group == s, r[s * VROWS : (s + 1) * VROWS], rows)
            rel_ref[pl.ds(i * VROWS * across + j, VROWS, stride=across), :] = rows
        return carry

    lax.fori_loop(0, height, body, 0, unroll=4)


def cell_rows(parts, place_ref):
    x = jnp.concatenate([x for part in parts for x in part], axis=0)
    hi = x.astype(BF16)
    r = mm(jnp.concatenate([hi, (x - hi.astype(F32)).astype(BF16)], axis=1), place_ref[...])
    out = []
    for n in range(len(parts)):
        for q in range(TROWS):
            out.append(
                pick_rows(
                    [
                        r[(n * 8 + u) * 8 : (n * 8 + u + 1) * 8, q * LANES : (q + 1) * LANES]
                        for u in range(8)
                    ]
                )
            )
    return out


def tile_kernel(height, across, capacity, per_owner, meta_ref, agg_ref, ret_ref, v_ref, inv_ref, place_ref,
                tile_ref, out_ref, ea_ref, eb_ref, ra_ref, rb_ref):
    hcount = -(-capacity // 4)
    group_lane = lane_iota(NC) // NV
    inv = inv_ref[...]

    def body(i, carry):
        for g in range(across // capacity):
            owner = lax.div(agg_ref[(i * across + g * capacity) * (KS + 1) + KS], per_owner)
            for h in range(hcount):
                m = ret_ref[pl.ds(pl.multiple_of((owner * hcount + h) * NC, NC), NC), :]
                m_hi = upper(m)
                left = jnp.concatenate(
                    [jnp.where(group_lane == s, x, 0.0) for x in (m_hi, m - m_hi) for s in range(4)],
                    axis=0,
                ).astype(BF16)
                upper_rows, lower_rows = [], []
                for s in range(4):
                    if h * 4 + s < capacity:
                        b = i * across + g * capacity + h * 4 + s
                        both = split(v_ref[pl.ds(b * NV, NV), :] * inv)
                    else:
                        both = jnp.zeros((2 * NV, LANES), BF16)
                    upper_rows.append(both[:NV])
                    lower_rows.append(both[NV:])
                r = mm(
                    jnp.concatenate([left, left], axis=1),
                    jnp.concatenate(upper_rows + lower_rows, axis=0),
                )
                for s in range(min(4, capacity - h * 4)):
                    t = r[s * NC : (s + 1) * NC] + r[(4 + s) * NC : (5 + s) * NC]
                    b = i * across + g * capacity + h * 4 + s
                    tile_ref[pl.ds(b * NC, NC), :] = t
        return carry

    lax.fori_loop(0, height, body, 0, unroll=2)
    step = 4 if height % 4 == 0 else 1

    def rows(s, carry):
        parts = [
            [tile_ref[pl.ds(((s * step + i) * across + j) * NC, NC), :] for j in range(across)]
            for i in range(step)
        ]
        for n, x in enumerate(cell_rows(parts, place_ref)):
            at = pl.multiple_of((s * step * TROWS + n) * across, 8)
            out_ref[pl.ds(at, across), :] = x
        return carry

    lax.fori_loop(0, height // step, rows, 0)
    row_a, row_b, col_a, col_b = halo_slots(meta_ref, height, across)

    def edge(i, carry):
        for ref, col in ((ea_ref, col_a), (eb_ref, col_b)):
            j = jnp.where(col == 0, 0, across - 1)
            ref[pl.ds(i * NC, NC), :] = tile_ref[pl.ds((i * across + j) * NC, NC), :]
        return carry

    lax.fori_loop(0, height, edge, 0)
    for ref, row in ((ra_ref, row_a), (rb_ref, row_b)):
        i = jnp.where(row == 0, 0, height - 1)
        ref[...] = tile_ref[pl.ds(pl.multiple_of(i * across * NC, 8), across * NC), :]


def product_kernel(height, across, near_ref, meta_ref, at_ref, tile_ref, pa_ref, pb_ref, sa_ref, sb_ref,
                   place_ref, out_ref, u_ref):
    wide = across + 2
    row_a, row_b, col_a, col_b = halo_slots(meta_ref, height, across)
    low = lane_iota(NC) < 64

    def put(index, x):
        hi = upper(x)
        lo = x - hi
        u_ref[index] = jnp.concatenate(
            [
                jnp.where(low, hi, 0.0), jnp.where(low, lo, 0.0),
                jnp.where(low, 0.0, hi), jnp.where(low, 0.0, lo),
            ],
            axis=0,
        ).astype(BF16)

    def own(i, carry):
        for j in range(across):
            put((i + 1) * wide + j + 1, tile_ref[pl.ds((i * across + j) * NC, NC), :])
        for ref, col in ((pa_ref, col_a), (pb_ref, col_b)):
            put((i + 1) * wide + col, ref[pl.ds(i * NC, NC), :])
        return carry

    lax.fori_loop(0, height, own, 0)
    for ref, row in ((sa_ref, row_a), (sb_ref, row_b)):
        for j in range(wide):
            col = j + 1 if j < across else (col_a if j == across else col_b)
            put(row * wide + col, ref[j * NC : (j + 1) * NC, :])

    def body(i, carry):
        parts = [[] for _ in range(KS)]
        for j in range(across):
            b = i * across + j
            u = [
                u_ref[neighbour(near_ref, b, i, j, k, wide), (k % 2) * 2 * NC : (k % 2 + 1) * 2 * NC, :]
                for k in range(KS)
            ]
            for t in range(3):
                left = jnp.concatenate(u[2 * t : 2 * t + 2], axis=0)
                if t < 2:
                    r = mm(left, at_ref[b, t * LANES : (t + 1) * LANES, :])
                else:
                    r = mm(left[:, :BLK], at_ref[b, 2 * LANES : 2 * LANES + BLK, :])
                for s in range(left.shape[0] // (2 * NC)):
                    parts[2 * t + s].append(
                        r[s * 2 * NC : s * 2 * NC + NC] + r[s * 2 * NC + NC : (s + 1) * 2 * NC]
                    )
        for n, rows in enumerate(cell_rows(parts, place_ref)):
            at = pl.multiple_of((i * KS * TROWS + n) * across, 8)
            out_ref[pl.ds(at, across), :] = rows
        return carry

    lax.fori_loop(0, height, body, 0, unroll=4)


def swaps(count, first):
    pairs = [(i, i + 1) for i in range(first, count - 1, 2)]
    return pairs + [(b, a) for a, b in pairs]


def exchange(edges, rows, slab_odd, unit, height, work=None):
    pencils, slabs = lax.axis_size("pencil"), lax.axis_size("slab")
    got = []
    for s, e in enumerate(edges):
        got.append(lax.ppermute(e, "pencil", swaps(pencils, s)))
    done = work() if work else None
    messages = []
    for s, own in enumerate(rows):
        last = (slab_odd == 0) if s == 0 else (slab_odd == 1)
        corners = [
            jnp.where(last, g[(height - 1) * unit : height * unit], g[:unit]) for g in got
        ]
        messages.append(jnp.concatenate([own] + corners, axis=0))
    if work:
        messages = [m + done[-1] for m in messages]
    out = []
    for s, m in enumerate(messages):
        out.append(lax.ppermute(m, "slab", swaps(slabs, s)))
    return got + out, messages, done


def lines(x, features):
    height, across, _ = x.shape
    y = x.reshape(height, across, features // LANES, LANES).transpose(0, 2, 1, 3)
    return y.reshape(height * across * features // LANES, LANES)


def unlines(y, height, across, features):
    x = y.reshape(height, features // LANES, across, LANES).transpose(0, 2, 1, 3)
    return x.reshape(height, across, features)


def call(kernel, outs, ins, scratch=(), limit=LIMIT, specs=None, aliases=None):
    return pl.pallas_call(
        kernel,
        out_shape=outs,
        in_specs=specs,
        out_specs=[VM] * len(outs),
        scratch_shapes=list(scratch),
        input_output_aliases=aliases or {},
        compiler_params=pltpu.CompilerParams(vmem_limit_bytes=limit),
    )(*ins)


def sds(*shape, dtype=F32):
    return jax.ShapeDtypeStruct(shape, dtype)


def mode_table():
    centre = np.arange(BLK, dtype=np.float64) + 0.5
    q = np.cos(math.pi * centre[:, None] * np.arange(NC)[None, :] / BLK).astype(np.float32)
    return q


def shards(a_blocks, col_codes, agg_of, test_vectors):
    height, across = agg_of.shape
    slabs, pencils = lax.axis_size("slab"), lax.axis_size("pencil")
    devices = slabs * pencils
    block_rows = height * across
    capacity = 2 * block_rows // devices
    per_owner = block_rows // 8
    hcount = -(-capacity // 4)
    wide = across + 2
    slab_odd = lax.axis_index("slab") % 2
    pencil_odd = lax.axis_index("pencil") % 2
    meta = jnp.stack([slab_odd, pencil_odd]).astype(jnp.int32)
    down = jnp.arange(height, dtype=jnp.int32)[:, None, None] + col_codes // 3
    near = down * wide + jnp.arange(across, dtype=jnp.int32)[None, :, None] + col_codes % 3
    ints = jnp.concatenate([near, agg_of[:, :, None]], axis=2).reshape(-1)

    tv = lines(test_vectors, BLK * NV)
    *edges, row_one, row_two = call(
        functools.partial(edge_kernel, height, across),
        [sds(height * VROWS, LANES)] * 2 + [sds(across * VROWS, LANES)] * 2,
        [meta, tv],
        specs=[SM, VM],
    )
    rows = [row_one, row_two]

    lane = np.arange(LANES)
    place_to = np.arange(TROWS * LANES) // NC
    place_one = ((lane[:, None] % BLK) == place_to[None, :]) & (lane[:, None] < BLK)
    place = jnp.asarray(np.concatenate([place_one, place_one], axis=0), BF16)
    stored = 2 * (lane % PAIRS) + lane // BLK
    place_one = stored[:, None] == place_to[None, :]
    place_stored = jnp.asarray(np.concatenate([place_one, place_one], axis=0), BF16)
    q = mode_table()
    q_hi = jnp.asarray(q.T).astype(BF16)
    q_lo = (jnp.asarray(q.T) - q_hi.astype(F32)).astype(BF16)
    modes = jnp.pad(jnp.concatenate([q_hi, q_lo], axis=1), ((0, NC), (0, 0)))

    chunk = KS * PAIRS * across
    stored_blocks = pltpu.with_memory_space_constraint(lines(a_blocks, KS * BLK * BLK), pltpu.HBM)

    def prepare(start, stop, earlier, after=()):
        count = 3 + len(after)
        return call(
            functools.partial(prepare_kernel, across, start, stop),
            [
                sds(block_rows, KS * BLK, LANES, dtype=BF16),
                sds(block_rows, LANES),
                sds(block_rows * NV, LANES),
            ],
            [ints, stored_blocks, tv, *after, *earlier],
            [
                pltpu.VMEM((4, chunk, LANES), F32),
                pltpu.VMEM((across, BLK, LANES), F32),
                pltpu.SemaphoreType.DMA((4,)),
            ],
            specs=[SM, HB, VM] + [HB] * len(after) + [VM] * len(earlier),
            aliases={count + n: n for n in range(len(earlier))},
        )

    halo, sent, _ = exchange(edges, rows, slab_odd, VROWS, height)
    at, rd, v = prepare(0, height, [], sent)
    field = [pltpu.VMEM((wide * (height + 2), 2 * NV, LANES), BF16)]
    v, ea, eb, ra, rb = call(
        functools.partial(sweep_kernel, height, across),
        [sds(block_rows * NV, LANES)] + [sds(height * VROWS, LANES)] * 2 + [sds(across * VROWS, LANES)] * 2,
        [ints, meta, at, rd, v, *halo],
        field + [pltpu.VMEM((across, BLK, LANES), F32)],
        specs=[SM, SM] + [VM] * 7,
    )
    outs = [
        sds(block_rows * NV, LANES),
        sds(wide * (height + 2), 2 * NV, LANES, dtype=BF16),
    ]
    halo, _, partial = exchange(
        [ea, eb], [ra, rb], slab_odd, VROWS, height,
        lambda: call(
            functools.partial(inner_sweep_kernel, height, across),
            outs + [sds(wide * VROWS, LANES)],
            [ints, meta, at, rd, v],
            specs=[SM, SM] + [VM] * 3,
        ),
    )
    slot_rows = hcount * NC + 1
    outs = outs + [sds(devices * slot_rows, LANES)]
    sizes = (height, across, capacity, per_owner)
    *partial, acc = call(
        functools.partial(side_sweep_kernel, *sizes),
        outs + [sds(NV, LANES)],
        [ints, meta, at, rd, v, *halo[:2], modes, *partial[:2]],
        specs=[SM, SM] + [VM] * 8,
        aliases={8: 0, 9: 1},
    )
    v, _, pay = call(
        functools.partial(outer_sweep_kernel, *sizes),
        outs,
        [ints, meta, at, rd, v, *halo[2:], modes, acc, *partial],
        specs=[SM, SM] + [VM] * 10,
        aliases={9: 0, 10: 1, 11: 2},
    )
    got = lax.all_to_all(
        pay.reshape(devices, slot_rows * LANES), ("slab", "pencil"), split_axis=0, concat_axis=0, tiled=True
    ).reshape(devices * slot_rows, LANES)
    ret, inv = call(
        functools.partial(solve_kernel, float(block_rows * BLK * devices), per_owner, capacity),
        [sds(devices * hcount * NC, LANES), sds(NV, LANES)],
        [got],
        specs=[VM],
    )
    back = lax.all_to_all(
        ret.reshape(devices, hcount * NC * LANES), ("slab", "pencil"), split_axis=0, concat_axis=0, tiled=True
    ).reshape(devices * hcount * NC, LANES)
    tile, tiles, ea, eb, ra, rb = call(
        functools.partial(tile_kernel, height, across, capacity, per_owner),
        [sds(block_rows * NC, LANES), sds(block_rows * TROWS, LANES)]
        + [sds(height * NC, LANES)] * 2 + [sds(across * NC, LANES)] * 2,
        [meta, ints, back, v, inv, place],
        specs=[SM, SM, VM, VM, VM, VM],
    )
    (relaxed,) = call(
        functools.partial(relaxed_kernel, height, across),
        [sds(block_rows * VROWS, LANES)],
        [v, inv, tile],
        specs=[VM] * 3,
    )
    halo, _, _ = exchange([ea, eb], [ra, rb], slab_odd, NC, height)
    (products,) = call(
        functools.partial(product_kernel, height, across),
        [sds(block_rows * KS * TROWS, LANES)],
        [ints, meta, at, tile, *halo, place_stored],
        [pltpu.VMEM((wide * (height + 2), 4 * NC, LANES), BF16)],
        specs=[SM, SM] + [VM] * 7,
    )
    return (
        unlines(relaxed, height, across, BLK * NV),
        unlines(tiles, height, across, BLK * NC),
        unlines(products, height, across, KS * BLK * NC),
    )


def solution(mesh):
    in_specs = (P("slab", "pencil", None), P("slab", "pencil", None), P("slab", "pencil"), P("slab", "pencil", None))
    out_specs = (P("slab", "pencil", None),) * 3
    return jax.shard_map(shards, mesh=mesh, in_specs=in_specs, out_specs=out_specs, check_vma=False)
```
